256 devices in a mesh: stn: 8 (over z), tm: 32 (over y, x, core).
Axes of the slice: x: 4, y: 4, z: 8, core: 2. Of those that a mesh axis runs over, the one named last changes fastest.
Arguments:
- voltages: bfloat16 [512, 2, 2, 256, 2048], P('tm', None, None, 'stn'), may hold values from -6 to 6
- taps: float32 [16, 2048], replicated, may hold values from -1.5 to 1.5
- sk_tolerance: float32 [384], P('tm'), may hold values from 0.05 to 0.3
- station_coords: int32 [256, 2], replicated, may hold values from 0 to 1023
- pointings: int32 [256, 2], replicated, may hold values from -64 to 64
- station_flags: int32 [256], replicated, may hold values 0 or 1
Outputs:
- beam_power: float32 [384, 32, 256], P('tm', None, 'stn')
The draws below stay inside these ranges and needn't reach their ends.
All inputs are finite; a program needn't handle non-finite values.
Results may differ from the reference program's by a relative error of at most 0.0045.
Values may be sent and summed in bfloat16 or wider, within the bound.
No kernel may reach another device: no remote copies, remote signals or barrier semaphores. Data moves between devices by JAX's collectives and lax.ppermute only.
A program may use at most 128 MiB of HBM per device.

```python
import math
import jax
import jax.numpy as jnp
from jax import lax

F_DEV = 16
STATIONS = 256
NFFT = 2048
CHAN = 384
TAPS = 16
BEAMS = 256
INTEG = 16
S_DEV = 32
FRAMES = 512
N_STN = 8


def plant(drawn, stream_key, low, largest):
    longest = drawn.shape.index(max(drawn.shape))
    spots = []
    for shift in (0, 1):
        where = [jax.random.randint(jax.random.fold_in(stream_key, axis), (), 0, length) for axis, length in enumerate(drawn.shape)]
        where[longest] = (where[longest] + shift) % drawn.shape[longest]
        spots.append(tuple(where))
    return drawn.at[spots[0]].set(low).at[spots[1]].set(largest)


def shard_levels(stream_key, extent, split, least, high):
    factor_of = 1.0
    for dim, blocks in split:
        steps = jax.random.uniform(jax.random.fold_in(jax.random.fold_in(stream_key, 6), dim), (blocks,), jnp.float32, least / len(split), high / len(split))
        factor_of = factor_of * jnp.repeat(jnp.exp(steps), extent[dim] // blocks).reshape((-1,) + (1,) * (len(extent) - 1 - dim))
    return factor_of


def bell_draw(own_key, extent, scale, most, pieces=(), kind=jnp.bfloat16):
    array = scale * jax.random.normal(own_key, extent, jnp.float32)
    if pieces:
        array = array * shard_levels(own_key, extent, pieces, -0.22, 0.18)
    return jnp.clip(array, -most, most).astype(kind)


def setup_inputs(seed: int = 0) -> dict:
    streams_of = jax.random.split(jax.random.key(seed), 7)
    voltages = bell_draw(streams_of[0], (FRAMES, 2, 2, STATIONS, NFFT), 1.0, 6.0, ((0, 32), (3, 8)))
    taps = bell_draw(streams_of[1], (TAPS, NFFT), TAPS ** -0.5, 1.5, (), jnp.float32)
    sk_tolerance = jnp.clip(jnp.exp(math.log(0.3) - 1.7917595 * jax.random.uniform(streams_of[2], (CHAN,), jnp.float32) ** shard_levels(streams_of[2], (CHAN,), ((0, 32),), -0.2, 0.2)), 0.05, 0.3)
    station_coords = plant(jax.random.randint(streams_of[3], (STATIONS, 2), 0, 1024), jax.random.fold_in(streams_of[3], 1), 0, 1023).astype(jnp.int32)
    pointings = plant(jax.random.randint(streams_of[4], (BEAMS, 2), -64, 65), jax.random.fold_in(streams_of[4], 1), -64, 64).astype(jnp.int32)
    station_flags = plant((jax.random.randint(streams_of[5], (STATIONS,), 0, 8) < 1).astype(jnp.int32), jax.random.fold_in(streams_of[5], 1), 0, 1)
    return {"voltages": voltages, "taps": taps, "sk_tolerance": sk_tolerance, "station_coords": station_coords, "pointings": pointings, "station_flags": station_flags}


def fourier_table(channels, points):
    rows = jnp.arange(channels, dtype=jnp.int32)
    columns = jnp.arange(points, dtype=jnp.int32)
    residue = rows[:, None] * columns[None, :] % points
    angle = 2.0 * math.pi / points * residue.astype(jnp.float32)
    factor = 1.0 / math.sqrt(points)
    return jnp.concatenate([jnp.cos(angle) * factor, jnp.sin(angle) * factor], 0).astype(jnp.bfloat16)

def steering(channel_ids, coords, flags, pointings, scale):
    offsets = coords[:, 0:1] * pointings[None, :, 0] + coords[:, 1:2] * pointings[None, :, 1]
    residue = (channel_ids + 1)[:, None, None] * offsets[None, :, :] % 65536
    angle = 2.0 * math.pi / 65536.0 * residue.astype(jnp.float32)
    live_gain = (1 - flags).astype(jnp.float32) * scale
    real_part = (jnp.cos(angle) * live_gain[None, :, None]).astype(jnp.bfloat16)
    imag_part = (jnp.sin(angle) * live_gain[None, :, None]).astype(jnp.bfloat16)
    upper = jnp.concatenate([real_part, imag_part], 2)
    lower = jnp.concatenate([-imag_part, real_part], 2)
    return jnp.stack([upper, lower], 1)

def own_sum(block, taps):
    frames = block.shape[0]
    span = taps.shape[0] - 1
    padded = jnp.pad(block, ((span, 0), (0, 0), (0, 0), (0, 0), (0, 0)))
    return sum((padded[span - tap_index:span - tap_index + frames].astype(jnp.float32) * taps[tap_index] for tap_index in range(taps.shape[0])))

def carried_sum(last_frames, taps):
    span = taps.shape[0] - 1
    padded = jnp.pad(last_frames, ((0, span), (0, 0), (0, 0), (0, 0), (0, 0)))
    return sum((padded[span - tap_index:2 * span - tap_index].astype(jnp.float32) * taps[tap_index] for tap_index in range(1, span + 1)))

def transform(filtered, table):
    frames = filtered.shape[0]
    local = filtered.shape[3]
    points = filtered.shape[-1]
    flat = filtered.reshape(-1, points)
    product = lax.dot_general(table, flat, (((1,), (1,)), ((), ())), preferred_element_type=jnp.float32)
    channels = table.shape[0] // 2
    product = product.reshape(2, channels, frames, 2, 2, local)
    real_out = product[0, :, :, 0] + product[1, :, :, 1]
    imag_out = product[0, :, :, 1] - product[1, :, :, 0]
    return jnp.stack([real_out, imag_out], 3)

def channelize(block, taps, table):
    span = taps.shape[0] - 1
    last_frames = block[:span]
    own_block = block[span:]
    own_part = transform(own_sum(own_block, taps).astype(jnp.bfloat16), table)
    carried_part = transform(carried_sum(last_frames, taps).astype(jnp.bfloat16), table)
    leading = own_part[:, :span] + carried_part
    return jnp.concatenate([leading, own_part[:, span:]], 1).astype(jnp.bfloat16)

def soft_weights(spectra, tolerance):
    count, frames, polars, parts, local = spectra.shape
    half = frames // 2
    values = spectra.astype(jnp.float32).reshape(count, 2, half, polars, parts, local)
    power = lax.optimization_barrier(jnp.sum(values * values, 4))
    first_sum = lax.optimization_barrier(jnp.sum(power, 2))
    second_sum = lax.optimization_barrier(jnp.sum(power * power, 2))
    size = float(half)
    kurtosis = (size + 1.0) / (size - 1.0) * (size * second_sum / (first_sum * first_sum) - 1.0)
    deviation = (kurtosis - 1.0) / tolerance[:, None, None, None]
    soft = 1.0 / (1.0 + deviation * deviation)
    weighted = values * soft[:, :, None, :, None, :]
    return weighted.astype(jnp.bfloat16).reshape(count, frames, polars, parts, local)

def reference(voltages, taps, sk_tolerance, station_coords, pointings, station_flags):
    frames_all = voltages.shape[0]
    span = TAPS - 1
    table = fourier_table(CHAN, NFFT)
    scale = 1.0 / math.sqrt(STATIONS)

    def one_block(index):
        own = lax.dynamic_slice_in_dim(voltages, index * F_DEV, F_DEV, 0)
        back = jnp.maximum(index * F_DEV - span, 0).astype(jnp.int32)
        prior = lax.dynamic_slice_in_dim(voltages, back, span, 0)
        prior = jnp.where(index > 0, prior, jnp.zeros_like(prior))
        return channelize(jnp.concatenate([prior, own], 0), taps, table)
    spectra = lax.map(one_block, jnp.arange(frames_all // F_DEV, dtype=jnp.int32))
    spectra = jnp.moveaxis(spectra, 0, 1).reshape(CHAN, frames_all, 2, 2, STATIONS)

    def one_channel(inputs):
        channel, values, tolerance = inputs
        weighted = soft_weights(values[None], tolerance[None])[0]
        weights = steering(channel[None], station_coords, station_flags, pointings, scale)[0]
        grouped = weighted.astype(jnp.float32).reshape(frames_all, 2, 2, N_STN, S_DEV)
        weight_groups = weights.astype(jnp.float32).reshape(2, N_STN, S_DEV, 2 * BEAMS)
        partial_value = jnp.einsum('tprgs,rgsj->gtpj', grouped, weight_groups)
        partial_value = lax.optimization_barrier(partial_value.astype(jnp.bfloat16)).astype(jnp.float32)
        beam = lax.optimization_barrier(jnp.sum(partial_value, 0))
        squares = (beam * beam).reshape(frames_all // INTEG, INTEG, 2, 2, BEAMS)
        return lax.optimization_barrier(jnp.sum(squares, (1, 2, 3))) / (2.0 * INTEG)
    return lax.map(one_channel, (jnp.arange(CHAN, dtype=jnp.int32), spectra, sk_tolerance))
```

```python
import functools
import math

import jax
import jax.numpy as jnp
import numpy as np
from jax import lax
from jax.experimental import pallas as pl
from jax.experimental.pallas import tpu as pltpu
from jax.sharding import PartitionSpec as P

STATIONS = 256
NFFT = 2048
CHAN = 384
BEAMS = 256
INTEG = 16
TAPS = 16
FRAMES = 16
N_STN = 8
N_TM = 32
S_DEV = 32
LOCAL_CHAN = CHAN // N_STN
OWNED = CHAN // N_TM
WINDOW = 16
RADIX = 4
POINTS = NFFT // RADIX
SEGS = 4
F32 = jnp.float32
BF16 = jnp.bfloat16

EVEN = (0, 4, 1, 5, 10, 11)
ODD = (2, 6, 3, 7, 8, 9)


def stn_of(offset, t):
    if offset in EVEN:
        return 2 * ((EVEN.index(offset) + t) % 4)
    return 2 * ((ODD.index(offset) + t) % 4) + 1


def slot_of(offset):
    return 1 if offset >= 8 else 0


def channel_plan():
    channels, slots, sizes = [], [], []
    for k in range(N_STN):
        mine, places, count = [], [], []
        for residue in range(RADIX):
            before = len(mine)
            for t in range(N_TM):
                for offset in range(residue, OWNED, RADIX):
                    if stn_of(offset, t) == k:
                        mine.append(OWNED * t + offset)
                        places.append(N_TM * slot_of(offset) + t)
            count.append(len(mine) - before)
        assert len(mine) == LOCAL_CHAN and len(set(places)) == LOCAL_CHAN
        assert all(n % 8 == 0 for n in count)
        channels.append(mine)
        slots.append(places)
        sizes.append(count)
    return channels, slots, sizes


CHANNELS, SLOTS, SIZES = channel_plan()
ORDER = [sorted(range(LOCAL_CHAN), key=lambda n, mine=mine: mine[n]) for mine in CHANNELS]
VISITED = [[mine[n] for n in order] for mine, order in zip(CHANNELS, ORDER)]
VISITED_SLOTS = [[places[n] for n in order] for places, order in zip(SLOTS, ORDER)]


def dft_tables():
    tables = []
    points = np.arange(POINTS)
    for residue in range(RADIX):
        order = []
        for k in range(N_STN):
            start = sum(SIZES[k][:residue])
            order += CHANNELS[k][start : start + SIZES[k][residue]]
        turns = (np.array(order)[:, None] * points[None, :]) % NFFT
        angle = 2.0 * np.pi * turns / NFFT
        cosine = np.cos(angle) / math.sqrt(NFFT)
        sine = np.sin(angle) / math.sqrt(NFFT)
        real_rows = np.stack([cosine, sine], 1)
        imag_rows = np.stack([-sine, cosine], 1)
        columns = np.zeros((2 * POINTS, 256))
        for part, rows in enumerate((real_rows, imag_rows)):
            rows = rows.reshape(-1, 2, POINTS // 128, 128).transpose(2, 1, 3, 0)
            columns[:, 128 * part : 128 * part + CHAN // RADIX] = rows.reshape(2 * POINTS, -1)
        tables.append(columns)
    return np.stack(tables, 0).astype(np.float32).astype(jnp.bfloat16)


def lane_permutation():
    source = np.arange(N_STN * 128)
    d, f4, s = source // 128, source // 32 % 4, source % 32
    target = f4 * STATIONS + d * S_DEV + s
    onehot = np.zeros((N_STN * 128, 4 * STATIONS), np.float32)
    onehot[source, target] = 1.0
    return onehot.astype(jnp.bfloat16)


def packed_sums(first, second):
    lane = lax.broadcasted_iota(jnp.int32, (LOCAL_CHAN, 128), 1)
    packed = None
    for group, total in enumerate((first[0], first[1], second[0], second[1])):
        total = total + pltpu.roll(total, 64, 1)
        total = total + pltpu.roll(total, 32, 1)
        packed = total if group == 0 else jnp.where(lane // 32 == group, total, packed)
    return packed


def channelize_kernel(carried, polar, *refs):
    if not carried:
        me_ref, refs = refs[0], refs[1:]
    v_refs, tap_refs, table_ref = refs[:RADIX], refs[RADIX : 2 * RADIX], refs[2 * RADIX]
    mixed, filtered, tables, arrival = refs[-4:]
    extra = refs[2 * RADIX + 1 : -4]
    if carried:
        (out_ref,) = extra
    elif polar == 0:
        received_ref, out_ref, sums_ref = extra
    else:
        received_ref, before_ref, tol_ref, out_ref, packed_ref, sums_ref = extra
    step = pl.program_id(0)
    outputs = FRAMES - 1 if carried else FRAMES
    load = pltpu.make_async_copy(table_ref, tables, arrival)

    @pl.when(step == 0)
    def _():
        load.start()

    def rows_chunk(chunk, _):
        row = pl.multiple_of(chunk * 16, 16)
        for j in range(RADIX):
            taps = [jnp.broadcast_to(tap_refs[j][k : k + 1, :], (16, 128)) for k in range(TAPS)]
            for r in range(2):
                x = [v_refs[j][f, r, 0, pl.ds(row, 16), :].astype(F32) for f in range(FRAMES)]
                for g in range(outputs):
                    if carried:
                        pairs = [(k, FRAMES + g - k) for k in range(g + 1, TAPS)]
                    else:
                        pairs = [(k, g - k) for k in range(g + 1)]
                    total = taps[pairs[0][0]] * x[pairs[0][1]]
                    for k, f in pairs[1:]:
                        total = total + taps[k] * x[f]
                    filtered[r, j, g] = total
        column = pl.multiple_of(step * 256, 256)
        for g in range(outputs):
            re = [filtered[0, j, g] for j in range(RADIX)]
            im = [filtered[1, j, g] for j in range(RADIX)]
            ar, ai = re[0] + re[2], im[0] + im[2]
            br, bi = re[0] - re[2], im[0] - im[2]
            cr, ci = re[1] + re[3], im[1] + im[3]
            dr, di = re[1] - re[3], im[1] - im[3]
            parts = (
                (ar + cr, ai + ci),
                (br + di, bi - dr),
                (ar - cr, ai - ci),
                (br - di, bi + dr),
            )
            target = pl.multiple_of(g * S_DEV + row, 16)
            for residue, (y_re, y_im) in enumerate(parts):
                mixed[residue, pl.ds(target, 16), pl.ds(column, 128)] = y_re.astype(BF16)
                mixed[residue, pl.ds(target, 16), pl.ds(column + 128, 128)] = y_im.astype(BF16)
        return 0

    lax.fori_loop(0, S_DEV // 16, rows_chunk, 0)

    @pl.when(step == pl.num_programs(0) - 1)
    def _():
        load.wait()
        if carried:
            for residue in range(RADIX):
                mixed[residue, outputs * S_DEV :, :] = jnp.zeros((S_DEV, 2 * POINTS), BF16)
        else:
            sums_ref[...] = jnp.zeros_like(sums_ref)
        for residue in range(RADIX):
            product = jnp.dot(mixed[residue], tables[residue], preferred_element_type=F32)
            for seg in range(SEGS):
                rows = product[seg * 128 : seg * 128 + 128]
                turned = (rows[:, :128].T, rows[:, 128:].T)
                row = 0
                for k in range(N_STN):
                    size = SIZES[k][residue]
                    start = sum(SIZES[k][:residue])
                    power = None
                    for part in range(2):
                        at = part * LOCAL_CHAN + start
                        piece = turned[part][row : row + size]
                        if not carried:
                            piece = piece + received_ref[k, seg, at : at + size, :].astype(F32)
                        piece = piece.astype(BF16)
                        out_ref[k, seg, at : at + size, :] = piece
                        if not carried:
                            value = piece.astype(F32)
                            power = value * value if power is None else power + value * value
                    if not carried:
                        place = lax.rem(k + N_STN - me_ref[0], N_STN)
                        sums_ref[place, 0, start : start + size, :] += power
                        sums_ref[place, 1, start : start + size, :] += power * power
                    row += size
        if not carried and polar == 1:
            for d in range(N_STN):
                packed_ref[d] = packed_sums(before_ref[d], sums_ref[d])
            packed_ref[N_STN] = tol_ref[...]


def channelize(voltages, taps, table, polar, received=None, me=None, before=None, tolerances=None):
    carried = received is None
    steps = POINTS // 128
    v_specs = [
        pl.BlockSpec((FRAMES, 2, 1, S_DEV, 128), functools.partial(lambda j, i: (0, 0, polar, 0, j * steps + i), j))
        for j in range(RADIX)
    ]
    t_specs = [
        pl.BlockSpec((TAPS, 128), functools.partial(lambda j, i: (0, j * steps + i), j)) for j in range(RADIX)
    ]
    whole = pl.BlockSpec(memory_space=pl.ANY)
    table = pltpu.with_memory_space_constraint(table, pltpu.HBM)
    vmem = pl.BlockSpec(memory_space=pltpu.VMEM)
    shape = jax.ShapeDtypeStruct((N_STN, SEGS, 2 * LOCAL_CHAN, 128), BF16)
    in_specs = v_specs + t_specs + [whole]
    voltages = pltpu.with_memory_space_constraint(voltages, pltpu.HBM)
    operands = [voltages] * RADIX + [taps] * RADIX + [table]
    outs, out_specs, scratch = [shape], [vmem], []
    if not carried:
        in_specs = [pl.BlockSpec(memory_space=pltpu.SMEM)] + in_specs + [vmem]
        operands = [me] + operands + [received]
        out_specs.append(vmem)
        if polar == 0:
            outs.append(jax.ShapeDtypeStruct((N_STN, 2, LOCAL_CHAN, 128), F32))
        else:
            in_specs += [vmem, vmem]
            operands += [before, tolerances]
            outs.append(jax.ShapeDtypeStruct((N_STN + 1, LOCAL_CHAN, 128), F32))
            scratch.append(pltpu.VMEM((N_STN, 2, LOCAL_CHAN, 128), F32))
    return pl.pallas_call(
        functools.partial(channelize_kernel, carried, polar),
        out_shape=outs,
        grid=(steps,),
        in_specs=in_specs,
        out_specs=out_specs,
        scratch_shapes=scratch
        + [
            pltpu.VMEM((RADIX, FRAMES * S_DEV, 2 * POINTS), BF16),
            pltpu.VMEM((2, RADIX, FRAMES, 16, 128), F32),
            pltpu.VMEM(table.shape, BF16),
            pltpu.SemaphoreType.DMA(()),
        ],
        compiler_params=pltpu.CompilerParams(
            dimension_semantics=("arbitrary",), vmem_limit_bytes=36 * 1024 * 1024
        ),
        cost_estimate=pl.CostEstimate(flops=12_000_000_000, bytes_accessed=8_000_000, transcendentals=0),
        name="carried" if carried else "own",
    )(*operands)


STATION_ROWS = 32


def turn(offsets, number):
    unit = 2.0 * math.pi / 65536.0
    residue = (offsets * number) & 65535
    quadrant = (residue + 8192) >> 14
    angle = (residue - (quadrant << 14)).astype(F32) * unit
    square = angle * angle
    sine = angle * (1.0 + square * (-1.0 / 6.0 + square * (1.0 / 120.0 - square * (1.0 / 5040.0))))
    cosine = 1.0 + square * (
        -0.5 + square * (1.0 / 24.0 + square * (-1.0 / 720.0 + square * (1.0 / 40320.0)))
    )
    odd = (quadrant & 1) == 1
    real = jnp.where(odd, sine, cosine)
    imag = jnp.where(odd, cosine, sine)
    real = jnp.where(((quadrant + 1) & 2) == 2, -real, real)
    imag = jnp.where((quadrant & 2) == 2, -imag, imag)
    return real, imag


def times(a, b):
    return a[0] * b[0] - a[1] * b[1], a[0] * b[1] + a[1] * b[0]


def steering_kernel(t_ref, o_ref, offset_ref, gain_ref, out_ref, coarse, fine):
    offsets = offset_ref[...]
    single = turn(offsets, 1)
    stride = turn(offsets, OWNED)
    fast = turn(offsets, 4 * OWNED)
    gain = gain_ref[...]
    value = (gain, jnp.zeros_like(gain))
    for t in range(4):
        coarse[t, 0], coarse[t, 1] = value
        if t < 3:
            value = times(value, stride)

    def advance(n, _):
        for i in range(4):
            t = 4 * n + i
            coarse[t, 0], coarse[t, 1] = times((coarse[t - 4, 0], coarse[t - 4, 1]), fast)
        return 0

    lax.fori_loop(1, N_TM // 4, advance, 0)
    pair = times(single, single)
    fine[0, 0], fine[0, 1] = single
    fine[1, 0], fine[1, 1] = pair
    for o in range(2, OWNED):
        fine[o, 0], fine[o, 1] = times((fine[o - 2, 0], fine[o - 2, 1]), pair)

    def channels(n, _):
        for i in range(4):
            at = 4 * n + i
            t, o = t_ref[at], o_ref[at]
            real, imag = times((coarse[t, 0], coarse[t, 1]), (fine[o, 0], fine[o, 1]))
            out_ref[at, :, :BEAMS] = real.astype(BF16)
            out_ref[at, :, BEAMS:] = imag.astype(BF16)
        return 0

    lax.fori_loop(0, LOCAL_CHAN // 4, channels, 0)


def steering(owners, places, offsets, gain):
    smem = pl.BlockSpec(memory_space=pltpu.SMEM)
    rows = pl.BlockSpec((STATION_ROWS, BEAMS), lambda i: (i, 0))
    return pl.pallas_call(
        steering_kernel,
        out_shape=jax.ShapeDtypeStruct((LOCAL_CHAN, STATIONS, 2 * BEAMS), BF16),
        grid=(STATIONS // STATION_ROWS,),
        in_specs=[smem, smem, rows, rows],
        out_specs=pl.BlockSpec((LOCAL_CHAN, STATION_ROWS, 2 * BEAMS), lambda i: (0, i, 0)),
        scratch_shapes=[
            pltpu.VMEM((N_TM, 2, STATION_ROWS, BEAMS), F32),
            pltpu.VMEM((OWNED, 2, STATION_ROWS, BEAMS), F32),
        ],
        compiler_params=pltpu.CompilerParams(
            dimension_semantics=("arbitrary",), vmem_limit_bytes=54 * 1024 * 1024
        ),
        cost_estimate=pl.CostEstimate(flops=40_000, bytes_accessed=12_600, transcendentals=0),
        name="steering",
    )(owners, places, offsets, gain)


def place_stations(in_ref, perm_ref, out_ref):
    for seg in range(SEGS):
        stacked = jnp.concatenate([in_ref[g, seg] for g in range(N_STN)], 1)
        moved = jnp.dot(stacked, perm_ref[...], preferred_element_type=F32)
        for part in range(2):
            rows = moved[part * LOCAL_CHAN : (part + 1) * LOCAL_CHAN]
            for f4 in range(4):
                at = ((part * 4 + f4) * SEGS + seg) * LOCAL_CHAN
                for half in range(2):
                    column = f4 * STATIONS + half * 128
                    out_ref[half, at : at + LOCAL_CHAN, :] = rows[:, column : column + 128]


PLACED = (2, 32 * LOCAL_CHAN, 128)


def gather(blocks, perm):
    vmem = pl.BlockSpec(memory_space=pltpu.VMEM)
    return pl.pallas_call(
        place_stations,
        out_shape=jax.ShapeDtypeStruct(PLACED, F32),
        in_specs=[vmem] * 2,
        out_specs=vmem,
        compiler_params=pltpu.CompilerParams(vmem_limit_bytes=8 * 1024 * 1024),
        cost_estimate=pl.CostEstimate(flops=800_000_000, bytes_accessed=4_000_000, transcendentals=0),
        name="stations",
    )(blocks, perm)


BLOCK = 8
CHUNKS = LOCAL_CHAN // BLOCK


def beam_kernel(me_ref, chan_ref, slot_ref, order_ref, tol_ref, *refs):
    sum_refs = refs[:N_STN]
    first_ref, second_ref, perm_ref, weight_ref, out_ref = refs[N_STN : N_STN + 5]
    window_sums, ordered, second_placed, weights, powers, arrival = refs[N_STN + 5 :]

    def load(chunk):
        part = pl.ds(chunk * BLOCK, BLOCK)
        return pltpu.make_async_copy(weight_ref.at[part], weights.at[part], arrival.at[chunk])

    for chunk in range(CHUNKS):
        load(chunk).start()
    place_stations(second_ref, perm_ref, second_placed)
    powers[...] = jnp.zeros_like(powers)
    lane = lax.broadcasted_iota(jnp.int32, (LOCAL_CHAN, 128), 1)
    for d in range(N_STN):
        ordered[lax.rem(me_ref[0] + N_STN - d, N_STN)] = sum_refs[d][...]
    for polar in range(2):
        for kind in range(2):
            group = 2 * polar + kind
            for half in range(2):
                total = jnp.zeros((LOCAL_CHAN, 128), F32)
                for place in range(4):
                    shift = 32 * ((place - group) % 4)
                    piece = ordered[4 * half + place]
                    if shift:
                        piece = pltpu.roll(piece, shift, 1)
                    total = jnp.where(lane // 32 == place, piece, total)
                window_sums[polar, kind, :, half * 128 : half * 128 + 128] = total

    size = float(WINDOW * FRAMES)

    def visit_chunk(chunk, _):
        load(chunk).wait()
        for inner in range(BLOCK):
            visit = chunk * BLOCK + inner
            local = order_ref[visit]
            tolerance = tol_ref[chan_ref[visit]]
            rows = []
            for polar, ref in enumerate((first_ref, second_placed)):
                s1 = window_sums[polar, 0, pl.ds(local, 1), :]
                s2 = window_sums[polar, 1, pl.ds(local, 1), :]
                kurtosis = (size + 1.0) / (size - 1.0) * (size * s2 / (s1 * s1) - 1.0)
                deviation = (kurtosis - 1.0) / tolerance
                soft = 1.0 / (1.0 + deviation * deviation)
                halves = [ref[half, pl.ds(local, 32, stride=LOCAL_CHAN), :] for half in range(2)]
                values = jnp.concatenate(halves, 1)
                rows.append((values * soft).astype(BF16))
            stacked = jnp.concatenate([rows[0][:16], rows[1][:16], rows[0][16:], rows[1][16:]], 0)
            product = jnp.dot(stacked, weights[visit], preferred_element_type=F32)
            real = product[:32, :BEAMS] - product[32:, BEAMS:]
            imag = product[:32, BEAMS:] + product[32:, :BEAMS]
            power = jnp.sum(real * real + imag * imag, 0, keepdims=True) * (1.0 / (2.0 * INTEG))
            powers[pl.ds(slot_ref[visit], 1), :] = power
        return 0

    lax.fori_loop(0, CHUNKS, visit_chunk, 0)
    share = BEAMS // N_STN
    out_ref[...] = jnp.zeros_like(out_ref)
    for slot in range(2):
        rows = powers[slot * N_TM : (slot + 1) * N_TM, :]
        for j in range(N_STN):
            out_ref[:, j, slot * share : (slot + 1) * share] = rows[:, j * share : (j + 1) * share]


def beams(me, channels, slots, order, tolerance, sums, first, second, perm, weights):
    smem = pl.BlockSpec(memory_space=pltpu.SMEM)
    vmem = pl.BlockSpec(memory_space=pltpu.VMEM)
    weights = pltpu.with_memory_space_constraint(weights, pltpu.HBM)
    return pl.pallas_call(
        beam_kernel,
        out_shape=jax.ShapeDtypeStruct((N_TM, N_STN, 128), F32),
        in_specs=[smem] * 5 + [vmem] * (N_STN + 3) + [pl.BlockSpec(memory_space=pl.ANY)],
        out_specs=vmem,
        scratch_shapes=[
            pltpu.VMEM((2, 2, LOCAL_CHAN, STATIONS), F32),
            pltpu.VMEM((N_STN, LOCAL_CHAN, 128), F32),
            pltpu.VMEM(PLACED, F32),
            pltpu.VMEM((LOCAL_CHAN, STATIONS, 2 * BEAMS), BF16),
            pltpu.VMEM((2 * N_TM, BEAMS), F32),
            pltpu.SemaphoreType.DMA((CHUNKS,)),
        ],
        compiler_params=pltpu.CompilerParams(vmem_limit_bytes=36 * 1024 * 1024),
        cost_estimate=pl.CostEstimate(flops=2_400_000_000, bytes_accessed=16_000_000, transcendentals=0),
        name="beams",
    )(me, channels, slots, order, tolerance, *sums, first, second, perm, weights)


def settle_kernel(t_ref, in_ref, out_ref):
    for offset in range(OWNED):
        group = EVEN if offset in EVEN else ODD
        parity = 0 if offset in EVEN else 1
        k = 2 * lax.rem(group.index(offset) + t_ref[0], 4) + parity
        column = slot_of(offset) * 32
        out_ref[offset] = in_ref[pl.ds(k, N_TM, stride=N_STN), :][:, column : column + 32]


def settle(t, arrived):
    vmem = pl.BlockSpec(memory_space=pltpu.VMEM)
    return pl.pallas_call(
        settle_kernel,
        out_shape=jax.ShapeDtypeStruct((OWNED, N_TM, BEAMS // N_STN), F32),
        in_specs=[pl.BlockSpec(memory_space=pltpu.SMEM), vmem],
        out_specs=vmem,
        name="settle",
    )(t, arrived)


def across_stations(blocks):
    return lax.all_to_all(blocks, "stn", split_axis=0, concat_axis=0, tiled=True)


def after(value, *others):
    return lax.optimization_barrier((value, *others))[0]


def permuted(block, axis, send_to):
    return lax.ppermute(block, axis, [(i, send_to(i)) for i in range(lax.axis_size(axis))])


def window_round(sums, bits):
    parts = [permuted(sums, "tm", lambda i, flip=flip: i ^ flip) for flip in (bits[0], bits[1], bits[0] | bits[1])]
    return (sums + parts[0]) + (parts[1] + parts[2])


def per_device(voltages, taps, sk_tolerance, station_coords, pointings, station_flags):
    stn = lax.axis_index("stn")
    tm = lax.axis_index("tm")
    me = jnp.reshape(stn, (1,)).astype(jnp.int32)
    table = jnp.asarray(dft_tables())
    perm = jnp.asarray(lane_permutation())
    shift = [(i, i + 1) for i in range(N_TM - 1)]

    visited = np.array(VISITED)
    plans = np.stack([visited, np.array(VISITED_SLOTS), np.array(ORDER), visited // OWNED, visited % OWNED], 1)
    plan = lax.dynamic_index_in_dim(jnp.asarray(plans.astype(np.int32)), stn, 0, False)
    channels, slots, order, owners, places = plan
    offsets = station_coords[:, 0:1] * pointings[None, :, 0] + station_coords[:, 1:2] * pointings[None, :, 1]
    live = (1 - station_flags).astype(F32) * (1.0 / math.sqrt(STATIONS))
    gain = jnp.broadcast_to(live[:, None], (STATIONS, BEAMS))

    (leaving0,) = channelize(voltages, taps, table, 0)
    received0 = lax.ppermute(leaving0, "tm", shift)
    partner = permuted(after(sk_tolerance, leaving0), "tm", lambda i: i ^ WINDOW)
    holder = jnp.arange(CHAN, dtype=jnp.int32) // OWNED
    tolerances = jnp.where(holder == tm, jnp.tile(sk_tolerance, N_TM), 0.0)
    tolerances = jnp.where(holder == (tm ^ WINDOW), jnp.tile(partner, N_TM), tolerances)
    tolerances = jnp.pad(tolerances.reshape(CHAN // 128, 128), ((0, LOCAL_CHAN - CHAN // 128), (0, 0)))

    (leaving1,) = channelize(after(voltages, leaving0), taps, table, 1)
    received1 = lax.ppermute(leaving1, "tm", shift)
    blocks0, sums0 = channelize(after(voltages, leaving1, tolerances), taps, table, 0, received0, me)
    arrived0 = across_stations(blocks0)
    blocks1, sums = channelize(after(voltages, blocks0), taps, table, 1, received1, me, sums0, tolerances)
    weights = steering(after(owners, blocks1), places, offsets, gain)
    arrived1 = across_stations(after(blocks1, weights))

    sums = window_round(after(sums, arrived0, weights), (1, 2))
    sums = window_round(sums, (4, 8))
    tolerance = sums[N_STN, : CHAN // 128].reshape(CHAN)
    window = [sums[0]] + [
        permuted(sums[d], "stn", lambda i, d=d: (i + d) % N_STN) for d in range(1, N_STN)
    ]
    first = gather(arrived0, perm)
    outgoing = beams(me, channels, slots, order, tolerance, window, first, arrived1, perm, weights)
    outgoing = outgoing.reshape(N_TM * N_STN, 1, 128)
    landed = lax.all_to_all(outgoing, ("tm", "stn"), split_axis=0, concat_axis=0, tiled=True)
    return settle(jnp.reshape(tm, (1,)).astype(jnp.int32), landed.reshape(N_TM * N_STN, 128))


def solution(mesh):
    in_specs = (P("tm", None, None, "stn", None), P(), P("tm"), P(), P(), P())
    out_specs = P("tm", None, "stn")
    return jax.shard_map(
        per_device, mesh=mesh, in_specs=in_specs, out_specs=out_specs, check_vma=False
    )
```

```python
import functools
import math

import jax
import jax.numpy as jnp
import numpy as np
from jax import lax
from jax.experimental import pallas as pl
from jax.experimental.pallas import tpu as pltpu
from jax.sharding import PartitionSpec as P

STATIONS = 256
NFFT = 2048
CHAN = 384
BEAMS = 256
INTEG = 16
TAPS = 16
FRAMES = 16
N_STN = 8
N_TM = 32
S_DEV = 32
LOCAL_CHAN = CHAN // N_STN
OWNED = CHAN // N_TM
WINDOW = 16
RADIX = 4
POINTS = NFFT // RADIX
SEGS = 4
F32 = jnp.float32
BF16 = jnp.bfloat16

EVEN = (0, 4, 1, 5, 10, 11)
ODD = (2, 6, 3, 7, 8, 9)


def stn_of(offset, t):
    if offset in EVEN:
        return 2 * ((EVEN.index(offset) + t) % 4)
    return 2 * ((ODD.index(offset) + t) % 4) + 1


def slot_of(offset):
    return 1 if offset >= 8 else 0


def channel_plan():
    channels, slots, sizes = [], [], []
    for k in range(N_STN):
        mine, places, count = [], [], []
        for residue in range(RADIX):
            before = len(mine)
            for t in range(N_TM):
                for offset in range(residue, OWNED, RADIX):
                    if stn_of(offset, t) == k:
                        mine.append(OWNED * t + offset)
                        places.append(N_TM * slot_of(offset) + t)
            count.append(len(mine) - before)
        assert len(mine) == LOCAL_CHAN and len(set(places)) == LOCAL_CHAN
        assert all(n % 8 == 0 for n in count)
        channels.append(mine)
        slots.append(places)
        sizes.append(count)
    return channels, slots, sizes


CHANNELS, SLOTS, SIZES = channel_plan()
ORDER = [sorted(range(LOCAL_CHAN), key=lambda n, mine=mine: mine[n]) for mine in CHANNELS]
VISITED = [[mine[n] for n in order] for mine, order in zip(CHANNELS, ORDER)]
assert all(c // OWNED // (N_TM // 2) == n // (LOCAL_CHAN // 2) for mine in VISITED for n, c in enumerate(mine))
VISITED_SLOTS = [[places[n] for n in order] for places, order in zip(SLOTS, ORDER)]


def dft_tables():
    tables = []
    points = np.arange(POINTS)
    for residue in range(RADIX):
        order = []
        for k in range(N_STN):
            start = sum(SIZES[k][:residue])
            order += CHANNELS[k][start : start + SIZES[k][residue]]
        turns = (np.array(order)[:, None] * points[None, :]) % NFFT
        angle = 2.0 * np.pi * turns / NFFT
        cosine = np.cos(angle) / math.sqrt(NFFT)
        sine = np.sin(angle) / math.sqrt(NFFT)
        real_rows = np.stack([cosine, sine], 1)
        imag_rows = np.stack([-sine, cosine], 1)
        columns = np.zeros((2 * POINTS, 256))
        for part, rows in enumerate((real_rows, imag_rows)):
            rows = rows.reshape(-1, 2, POINTS // 128, 128).transpose(2, 1, 3, 0)
            columns[:, 128 * part : 128 * part + CHAN // RADIX] = rows.reshape(2 * POINTS, -1)
        tables.append(columns)
    return np.stack(tables, 0).astype(np.float32).astype(jnp.bfloat16)


def lane_permutation():
    source = np.arange(N_STN * 128)
    d, f4, s = source // 128, source // 32 % 4, source % 32
    target = f4 * STATIONS + d * S_DEV + s
    onehot = np.zeros((N_STN * 128, 4 * STATIONS), np.float32)
    onehot[source, target] = 1.0
    return onehot.astype(jnp.bfloat16)


ROWS = FRAMES * S_DEV


def channelize_kernel(carried, *refs):
    v_refs, tap_refs, table_ref, out_ref = refs[:RADIX], refs[RADIX : 2 * RADIX], refs[2 * RADIX], refs[2 * RADIX + 1]
    mixed, filtered, spectra, tables, arrival = refs[2 * RADIX + 2 :]
    step = pl.program_id(0)
    outputs = FRAMES - 1 if carried else FRAMES
    load = pltpu.make_async_copy(table_ref, tables, arrival)

    @pl.when(step == 0)
    def _():
        load.start()

    def rows_chunk(chunk, _):
        polar = chunk // 2
        row = pl.multiple_of(chunk % 2 * 16, 16)
        for j in range(RADIX):
            taps = [jnp.broadcast_to(tap_refs[j][k : k + 1, :], (16, 128)) for k in range(TAPS)]
            for r in range(2):
                x = [v_refs[j][f, r, polar, pl.ds(row, 16), :].astype(F32) for f in range(FRAMES)]
                for g in range(outputs):
                    if carried:
                        pairs = [(k, FRAMES + g - k) for k in range(g + 1, TAPS)]
                    else:
                        pairs = [(k, g - k) for k in range(g + 1)]
                    total = taps[pairs[0][0]] * x[pairs[0][1]]
                    for k, f in pairs[1:]:
                        total = total + taps[k] * x[f]
                    filtered[r, j, g] = total
        column = pl.multiple_of(step * 256, 256)
        for g in range(outputs):
            re = [filtered[0, j, g] for j in range(RADIX)]
            im = [filtered[1, j, g] for j in range(RADIX)]
            ar, ai = re[0] + re[2], im[0] + im[2]
            br, bi = re[0] - re[2], im[0] - im[2]
            cr, ci = re[1] + re[3], im[1] + im[3]
            dr, di = re[1] - re[3], im[1] - im[3]
            parts = (
                (ar + cr, ai + ci),
                (br + di, bi - dr),
                (ar - cr, ai - ci),
                (br - di, bi + dr),
            )
            target = pl.multiple_of(polar * ROWS + g * S_DEV + row, 16)
            for residue, (y_re, y_im) in enumerate(parts):
                mixed[residue, pl.ds(target, 16), pl.ds(column, 128)] = y_re.astype(BF16)
                mixed[residue, pl.ds(target, 16), pl.ds(column + 128, 128)] = y_im.astype(BF16)
        return 0

    lax.fori_loop(0, 2 * (S_DEV // 16), rows_chunk, 0)

    @pl.when(step == pl.num_programs(0) - 1)
    def _():
        load.wait()
        if carried:
            for residue in range(RADIX):
                for polar in range(2):
                    last = polar * ROWS + outputs * S_DEV
                    mixed[residue, last : last + S_DEV, :] = jnp.zeros((S_DEV, 2 * POINTS), BF16)
        for residue in range(RADIX):
            product = jnp.dot(mixed[residue], tables[residue], preferred_element_type=F32)
            for seg in range(2 * SEGS):
                rows = product[seg * 128 : seg * 128 + 128]
                spectra[residue, 0, seg] = rows[:, :128].T
                spectra[residue, 1, seg] = rows[:, 128:].T
        for k in range(N_STN):
            rows = [sum(SIZES[n][residue] for n in range(k)) for residue in range(RADIX)]
            for seg in range(2 * SEGS):
                for part in range(2):
                    piece = jnp.concatenate(
                        [
                            spectra[residue, part, seg, rows[residue] : rows[residue] + SIZES[k][residue]]
                            for residue in range(RADIX)
                        ],
                        0,
                    )
                    at = slice(part * LOCAL_CHAN, (part + 1) * LOCAL_CHAN)
                    out_ref[k, seg, at] = piece.astype(out_ref.dtype)


BLOCKS = (N_STN, 2 * SEGS, 2 * LOCAL_CHAN, 128)


def channelize(voltages, taps, table, carried):
    steps = POINTS // 128
    v_specs = [
        pl.BlockSpec((FRAMES, 2, 2, S_DEV, 128), functools.partial(lambda j, i: (0, 0, 0, 0, j * steps + i), j))
        for j in range(RADIX)
    ]
    t_specs = [
        pl.BlockSpec((TAPS, 128), functools.partial(lambda j, i: (0, j * steps + i), j)) for j in range(RADIX)
    ]
    voltages, taps, table = (pltpu.with_memory_space_constraint(x, pltpu.HBM) for x in (voltages, taps, table))
    return pl.pallas_call(
        functools.partial(channelize_kernel, carried),
        out_shape=jax.ShapeDtypeStruct(BLOCKS, BF16 if carried else F32),
        grid=(steps,),
        in_specs=v_specs + t_specs + [pl.BlockSpec(memory_space=pl.ANY)],
        out_specs=pl.BlockSpec(memory_space=pltpu.VMEM),
        scratch_shapes=[
            pltpu.VMEM((RADIX, 2 * ROWS, 2 * POINTS), BF16),
            pltpu.VMEM((2, RADIX, FRAMES, 16, 128), F32),
            pltpu.VMEM((RADIX, 2, 2 * SEGS, 128, 128), F32),
            pltpu.VMEM(table.shape, BF16),
            pltpu.SemaphoreType.DMA(()),
        ],
        compiler_params=pltpu.CompilerParams(
            dimension_semantics=("arbitrary",), vmem_limit_bytes=40 * 1024 * 1024
        ),
        cost_estimate=pl.CostEstimate(flops=14_000_000_000, bytes_accessed=16_000_000, transcendentals=0),
        name="carried" if carried else "own",
    )(*([voltages] * RADIX), *([taps] * RADIX), table)


def combine_kernel(me_ref, own_ref, received_ref, tol_ref, out_ref, packed_ref, spectra, leaving):
    lane = lax.broadcasted_iota(jnp.int32, (LOCAL_CHAN, 128), 1)
    for k in range(N_STN):
        packed = None
        for polar in range(2):
            first = second = None
            for seg in range(polar * SEGS, (polar + 1) * SEGS):
                value = (own_ref[k, seg] + received_ref[k, seg].astype(F32)).astype(BF16)
                spectra[k, seg] = value
                value = value.astype(F32)
                power = value[:LOCAL_CHAN] * value[:LOCAL_CHAN] + value[LOCAL_CHAN:] * value[LOCAL_CHAN:]
                square = power * power
                first = power if first is None else first + power
                second = square if second is None else second + square
            for kind, total in enumerate((first, second)):
                total = total + pltpu.roll(total, 64, 1)
                total = total + pltpu.roll(total, 32, 1)
                group = 2 * polar + kind
                packed = total if group == 0 else jnp.where(lane // 32 == group, total, packed)
        pltpu.make_async_copy(spectra.at[k], out_ref.at[k], leaving.at[k]).start()
        packed_ref[lax.rem(k + N_STN - me_ref[0], N_STN)] = packed
    packed_ref[N_STN] = tol_ref[...]
    for k in range(N_STN):
        pltpu.make_async_copy(spectra.at[k], out_ref.at[k], leaving.at[k]).wait()


def combine(me, own, received, tolerances):
    vmem = pl.BlockSpec(memory_space=pltpu.VMEM)
    return pl.pallas_call(
        combine_kernel,
        out_shape=[
            jax.ShapeDtypeStruct(BLOCKS, BF16),
            jax.ShapeDtypeStruct((N_STN + 1, LOCAL_CHAN, 128), F32),
        ],
        in_specs=[pl.BlockSpec(memory_space=pltpu.SMEM), vmem, vmem, vmem],
        out_specs=[pl.BlockSpec(memory_space=pltpu.HBM), vmem],
        scratch_shapes=[pltpu.VMEM(BLOCKS, BF16), pltpu.SemaphoreType.DMA((N_STN,))],
        compiler_params=pltpu.CompilerParams(vmem_limit_bytes=16 * 1024 * 1024),
        cost_estimate=pl.CostEstimate(flops=8_000_000, bytes_accessed=8_000_000, transcendentals=0),
        name="combine",
    )(me, own, received, tolerances)


STATION_ROWS = 32


def turn(offsets, number):
    unit = 2.0 * math.pi / 65536.0
    residue = (offsets * number) & 65535
    quadrant = (residue + 8192) >> 14
    angle = (residue - (quadrant << 14)).astype(F32) * unit
    square = angle * angle
    sine = angle * (1.0 + square * (-1.0 / 6.0 + square * (1.0 / 120.0 - square * (1.0 / 5040.0))))
    cosine = 1.0 + square * (
        -0.5 + square * (1.0 / 24.0 + square * (-1.0 / 720.0 + square * (1.0 / 40320.0)))
    )
    odd = (quadrant & 1) == 1
    real = jnp.where(odd, sine, cosine)
    imag = jnp.where(odd, cosine, sine)
    real = jnp.where(((quadrant + 1) & 2) == 2, -real, real)
    imag = jnp.where((quadrant & 2) == 2, -imag, imag)
    return real, imag


def times(a, b):
    return a[0] * b[0] - a[1] * b[1], a[0] * b[1] + a[1] * b[0]


def steering_kernel(start, t_ref, o_ref, offset_ref, gain_ref, out_ref, coarse, fine):
    offsets = offset_ref[...]
    single = turn(offsets, 1)
    pair = times(single, single)
    fine[0, 0], fine[0, 1] = single
    fine[1, 0], fine[1, 1] = pair
    for o in range(2, OWNED):
        fine[o, 0], fine[o, 1] = times((fine[o - 2, 0], fine[o - 2, 1]), pair)
    stride = (fine[OWNED - 1, 0], fine[OWNED - 1, 1])
    double = times(stride, stride)
    fast = times(double, double)
    gain = gain_ref[...]
    value = (gain, jnp.zeros_like(gain))
    if start:
        value = tuple(part * gain for part in turn(offsets, OWNED * start))
    for t in range(4):
        coarse[t, 0], coarse[t, 1] = value
        if t < 3:
            value = times(value, stride)
    for t in range(4, N_TM // 2):
        coarse[t, 0], coarse[t, 1] = times((coarse[t - 4, 0], coarse[t - 4, 1]), fast)

    def channels(n, _):
        for i in range(4):
            at = 4 * n + i
            t, o = t_ref[at] - start, o_ref[at]
            real, imag = times((coarse[t, 0], coarse[t, 1]), (fine[o, 0], fine[o, 1]))
            out_ref[at, :, :BEAMS] = real.astype(BF16)
            out_ref[at, :, BEAMS:] = imag.astype(BF16)
        return 0

    lax.fori_loop(0, HALF // 4, channels, 0)


HALF = LOCAL_CHAN // 2


def steering(start, owners, places, offsets, gain):
    smem = pl.BlockSpec(memory_space=pltpu.SMEM)
    rows = pl.BlockSpec((STATION_ROWS, BEAMS), lambda i: (i, 0))
    return pl.pallas_call(
        functools.partial(steering_kernel, start),
        out_shape=jax.ShapeDtypeStruct((HALF, STATIONS, 2 * BEAMS), BF16),
        grid=(STATIONS // STATION_ROWS,),
        in_specs=[smem, smem, rows, rows],
        out_specs=pl.BlockSpec((HALF, STATION_ROWS, 2 * BEAMS), lambda i: (0, i, 0)),
        scratch_shapes=[
            pltpu.VMEM((N_TM // 2, 2, STATION_ROWS, BEAMS), F32),
            pltpu.VMEM((OWNED, 2, STATION_ROWS, BEAMS), F32),
        ],
        compiler_params=pltpu.CompilerParams(
            dimension_semantics=("arbitrary",), vmem_limit_bytes=54 * 1024 * 1024
        ),
        cost_estimate=pl.CostEstimate(flops=40_000, bytes_accessed=12_600, transcendentals=0),
        name="steering",
    )(owners, places, offsets, gain)


def place_stations(in_ref, polar, perm_ref, out_ref):
    for seg in range(SEGS):
        stacked = jnp.concatenate([in_ref[g, polar * SEGS + seg] for g in range(N_STN)], 1)
        moved = jnp.dot(stacked, perm_ref[...], preferred_element_type=F32)
        for part in range(2):
            rows = moved[part * LOCAL_CHAN : (part + 1) * LOCAL_CHAN]
            for f4 in range(4):
                at = ((part * 4 + f4) * SEGS + seg) * LOCAL_CHAN
                for half in range(2):
                    column = f4 * STATIONS + half * 128
                    out_ref[half, at : at + LOCAL_CHAN, :] = rows[:, column : column + 128]


PLACED = (2, 32 * LOCAL_CHAN, 128)


BLOCK = 8
CHUNKS = LOCAL_CHAN // BLOCK


def beam_kernel(me_ref, chan_ref, slot_ref, order_ref, tol_ref, *refs):
    sum_refs = refs[:N_STN]
    in_ref, perm_ref, low_ref, high_ref, out_ref = refs[N_STN : N_STN + 5]
    window_sums, ordered, first_placed, second_placed, perm, weights, powers, arrival = refs[N_STN + 5 :]

    def load(chunk):
        source, at = (low_ref, chunk) if chunk < CHUNKS // 2 else (high_ref, chunk - CHUNKS // 2)
        return pltpu.make_async_copy(
            source.at[pl.ds(at * BLOCK, BLOCK)], weights.at[pl.ds(chunk * BLOCK, BLOCK)], arrival.at[chunk]
        )

    load_perm = pltpu.make_async_copy(perm_ref, perm, arrival.at[CHUNKS])
    load_perm.start()
    for chunk in range(CHUNKS):
        load(chunk).start()
    powers[...] = jnp.zeros_like(powers)
    lane = lax.broadcasted_iota(jnp.int32, (LOCAL_CHAN, 128), 1)
    for d in range(N_STN):
        ordered[lax.rem(me_ref[0] + N_STN - d, N_STN)] = sum_refs[d][...]
    for polar in range(2):
        for kind in range(2):
            group = 2 * polar + kind
            for half in range(2):
                total = jnp.zeros((LOCAL_CHAN, 128), F32)
                for place in range(4):
                    shift = 32 * ((place - group) % 4)
                    piece = ordered[4 * half + place]
                    if shift:
                        piece = pltpu.roll(piece, shift, 1)
                    total = jnp.where(lane // 32 == place, piece, total)
                window_sums[polar, kind, :, half * 128 : half * 128 + 128] = total
    load_perm.wait()
    place_stations(in_ref, 0, perm, first_placed)
    place_stations(in_ref, 1, perm, second_placed)

    size = float(WINDOW * FRAMES)

    for chunk in range(CHUNKS):
        load(chunk).wait()
        for inner in range(BLOCK):
            visit = chunk * BLOCK + inner
            local = order_ref[visit]
            tolerance = tol_ref[chan_ref[visit]]
            rows = []
            for polar, ref in enumerate((first_placed, second_placed)):
                s1 = window_sums[polar, 0, pl.ds(local, 1), :]
                s2 = window_sums[polar, 1, pl.ds(local, 1), :]
                kurtosis = (size + 1.0) / (size - 1.0) * (size * s2 / (s1 * s1) - 1.0)
                deviation = (kurtosis - 1.0) / tolerance
                soft = 1.0 / (1.0 + deviation * deviation)
                halves = [ref[half, pl.ds(local, 32, stride=LOCAL_CHAN), :] for half in range(2)]
                values = jnp.concatenate(halves, 1)
                rows.append((values * soft).astype(BF16))
            stacked = jnp.concatenate([rows[0][:16], rows[1][:16], rows[0][16:], rows[1][16:]], 0)
            product = jnp.dot(stacked, weights[visit], preferred_element_type=F32)
            real = product[:32, :BEAMS] - product[32:, BEAMS:]
            imag = product[:32, BEAMS:] + product[32:, :BEAMS]
            power = jnp.sum(real * real + imag * imag, 0, keepdims=True) * (1.0 / (2.0 * INTEG))
            powers[pl.ds(slot_ref[visit], 1), :] = power

    share = BEAMS // N_STN
    out_ref[...] = jnp.zeros_like(out_ref)
    for slot in range(2):
        rows = powers[slot * N_TM : (slot + 1) * N_TM, :]
        for j in range(N_STN):
            out_ref[:, j, slot * share : (slot + 1) * share] = rows[:, j * share : (j + 1) * share]


def beams(me, channels, slots, order, tolerance, sums, arrived, perm, low, high):
    smem = pl.BlockSpec(memory_space=pltpu.SMEM)
    vmem = pl.BlockSpec(memory_space=pltpu.VMEM)
    low, high, perm = (pltpu.with_memory_space_constraint(x, pltpu.HBM) for x in (low, high, perm))
    return pl.pallas_call(
        beam_kernel,
        out_shape=jax.ShapeDtypeStruct((N_TM, N_STN, 128), F32),
        in_specs=[smem] * 5 + [vmem] * (N_STN + 1) + [pl.BlockSpec(memory_space=pl.ANY)] * 3,
        out_specs=vmem,
        scratch_shapes=[
            pltpu.VMEM((2, 2, LOCAL_CHAN, STATIONS), F32),
            pltpu.VMEM((N_STN, LOCAL_CHAN, 128), F32),
            pltpu.VMEM(PLACED, F32),
            pltpu.VMEM(PLACED, F32),
            pltpu.VMEM(perm.shape, BF16),
            pltpu.VMEM((LOCAL_CHAN, STATIONS, 2 * BEAMS), BF16),
            pltpu.VMEM((2 * N_TM, BEAMS), F32),
            pltpu.SemaphoreType.DMA((CHUNKS + 1,)),
        ],
        compiler_params=pltpu.CompilerParams(vmem_limit_bytes=36 * 1024 * 1024),
        cost_estimate=pl.CostEstimate(flops=2_400_000_000, bytes_accessed=16_000_000, transcendentals=0),
        name="beams",
    )(me, channels, slots, order, tolerance, *sums, arrived, perm, low, high)


def settle_kernel(t_ref, in_ref, out_ref):
    for offset in range(OWNED):
        group = EVEN if offset in EVEN else ODD
        parity = 0 if offset in EVEN else 1
        k = 2 * lax.rem(group.index(offset) + t_ref[0], 4) + parity
        column = slot_of(offset) * 32
        out_ref[offset] = in_ref[pl.ds(k, N_TM, stride=N_STN), :][:, column : column + 32]


def settle(t, arrived):
    vmem = pl.BlockSpec(memory_space=pltpu.VMEM)
    return pl.pallas_call(
        settle_kernel,
        out_shape=jax.ShapeDtypeStruct((OWNED, N_TM, BEAMS // N_STN), F32),
        in_specs=[pl.BlockSpec(memory_space=pltpu.SMEM), vmem],
        out_specs=vmem,
        name="settle",
    )(t, arrived)


def across_stations(blocks):
    return lax.all_to_all(blocks, "stn", split_axis=0, concat_axis=0, tiled=True)


def after(value, *others):
    return lax.optimization_barrier((value, *others))[0]


def permuted(block, axis, send_to):
    return lax.ppermute(block, axis, [(i, send_to(i)) for i in range(lax.axis_size(axis))])


def window_round(sums, bits):
    parts = [permuted(sums, "tm", lambda i, flip=flip: i ^ flip) for flip in (bits[0], bits[1], bits[0] | bits[1])]
    return (sums + parts[0]) + (parts[1] + parts[2])


def per_device(voltages, taps, sk_tolerance, station_coords, pointings, station_flags):
    stn = lax.axis_index("stn")
    tm = lax.axis_index("tm")
    me = jnp.reshape(stn, (1,)).astype(jnp.int32)
    table = jnp.asarray(dft_tables())
    perm = jnp.asarray(lane_permutation())
    shift = [(i, i + 1) for i in range(N_TM - 1)]

    visited = np.array(VISITED)
    plans = np.stack([visited, np.array(VISITED_SLOTS), np.array(ORDER), visited // OWNED, visited % OWNED], 1)
    plan = lax.dynamic_index_in_dim(jnp.asarray(plans.astype(np.int32)), stn, 0, False)
    channels, slots, order, owners, places = plan
    offsets = station_coords[:, 0:1] * pointings[None, :, 0] + station_coords[:, 1:2] * pointings[None, :, 1]
    live = (1 - station_flags).astype(F32) * (1.0 / math.sqrt(STATIONS))
    gain = jnp.broadcast_to(live[:, None], (STATIONS, BEAMS))

    leaving = channelize(voltages, taps, table, True)
    received = lax.ppermute(leaving, "tm", shift)
    holder = jnp.arange(CHAN, dtype=jnp.int32) // OWNED
    tolerances = jnp.where(holder == tm, jnp.tile(sk_tolerance, N_TM), 0.0)
    tolerances = jnp.pad(tolerances.reshape(CHAN // 128, 128), ((0, LOCAL_CHAN - CHAN // 128), (0, 0)))

    own = channelize(after(voltages, leaving), taps, table, False)
    blocks, sums = combine(me, own, received, tolerances)
    arrived = across_stations(blocks)
    sums = window_round(sums, (1, 2))
    low = steering(0, after(owners[:HALF], blocks), places[:HALF], offsets, gain)
    sums = window_round(after(sums, low), (4, 8))
    high = steering(N_TM // 2, after(owners[HALF:], low), places[HALF:], offsets, gain)
    sums = after(sums, high)
    tolerance = sums[N_STN, :8]
    tolerance = tolerance + permuted(tolerance, "tm", lambda i: i ^ WINDOW)
    tolerance = tolerance[: CHAN // 128].reshape(CHAN)
    window = [sums[0]] + [
        permuted(sums[d], "stn", lambda i, d=d: (i + d) % N_STN) for d in range(1, N_STN)
    ]
    outgoing = beams(me, channels, slots, order, tolerance, window, arrived, perm, low, high)
    outgoing = outgoing.reshape(N_TM * N_STN, 1, 128)
    landed = lax.all_to_all(outgoing, ("tm", "stn"), split_axis=0, concat_axis=0, tiled=True)
    return settle(jnp.reshape(tm, (1,)).astype(jnp.int32), landed.reshape(N_TM * N_STN, 128))


def solution(mesh):
    in_specs = (P("tm", None, None, "stn", None), P(), P("tm"), P(), P(), P())
    out_specs = P("tm", None, "stn")
    return jax.shard_map(
        per_device, mesh=mesh, in_specs=in_specs, out_specs=out_specs, check_vma=False
    )
```

```python
import functools
import math

import jax
import jax.numpy as jnp
import numpy as np
from jax import lax
from jax.experimental import pallas as pl
from jax.experimental.pallas import tpu as pltpu
from jax.sharding import PartitionSpec as P

STATIONS = 256
NFFT = 2048
CHAN = 384
BEAMS = 256
INTEG = 16
TAPS = 16
FRAMES = 16
N_STN = 8
N_TM = 32
S_DEV = 32
LOCAL_CHAN = CHAN // N_STN
OWNED = CHAN // N_TM
WINDOW = 16
RADIX = 4
POINTS = NFFT // RADIX
SEGS = 4
F32 = jnp.float32
BF16 = jnp.bfloat16

EVEN = (0, 4, 1, 5, 10, 11)
ODD = (2, 6, 3, 7, 8, 9)


def stn_of(offset, t):
    if offset in EVEN:
        return 2 * ((EVEN.index(offset) + t) % 4)
    return 2 * ((ODD.index(offset) + t) % 4) + 1


def slot_of(offset):
    return 1 if offset >= 8 else 0


def channel_plan():
    channels, slots, sizes = [], [], []
    for k in range(N_STN):
        mine, places, count = [], [], []
        for residue in range(RADIX):
            before = len(mine)
            for t in range(N_TM):
                for offset in range(residue, OWNED, RADIX):
                    if stn_of(offset, t) == k:
                        mine.append(OWNED * t + offset)
                        places.append(N_TM * slot_of(offset) + t)
            count.append(len(mine) - before)
        assert len(mine) == LOCAL_CHAN and len(set(places)) == LOCAL_CHAN
        assert all(n % 8 == 0 for n in count)
        channels.append(mine)
        slots.append(places)
        sizes.append(count)
    return channels, slots, sizes


CHANNELS, SLOTS, SIZES = channel_plan()
ORDER = [sorted(range(LOCAL_CHAN), key=lambda n, mine=mine: mine[n]) for mine in CHANNELS]
VISITED = [[mine[n] for n in order] for mine, order in zip(CHANNELS, ORDER)]
assert all(c // OWNED // (N_TM // 2) == n // (LOCAL_CHAN // 2) for mine in VISITED for n, c in enumerate(mine))
VISITED_SLOTS = [[places[n] for n in order] for places, order in zip(SLOTS, ORDER)]


def dft_tables():
    tables = []
    points = np.arange(POINTS)
    for residue in range(RADIX):
        order = []
        for k in range(N_STN):
            start = sum(SIZES[k][:residue])
            order += CHANNELS[k][start : start + SIZES[k][residue]]
        turns = (np.array(order)[:, None] * points[None, :]) % NFFT
        angle = 2.0 * np.pi * turns / NFFT
        cosine = np.cos(angle) / math.sqrt(NFFT)
        sine = np.sin(angle) / math.sqrt(NFFT)
        real_rows = np.stack([cosine, sine], 1)
        imag_rows = np.stack([-sine, cosine], 1)
        columns = np.zeros((2 * POINTS, 256))
        for part, rows in enumerate((real_rows, imag_rows)):
            rows = rows.reshape(-1, 2, POINTS // 128, 128).transpose(2, 1, 3, 0)
            columns[:, 128 * part : 128 * part + CHAN // RADIX] = rows.reshape(2 * POINTS, -1)
        tables.append(columns)
    return np.stack(tables, 0).astype(np.float32).astype(jnp.bfloat16)


def lane_permutation():
    source = np.arange(N_STN * 128)
    d, f4, s = source // 128, source // 32 % 4, source % 32
    target = f4 * STATIONS + d * S_DEV + s
    onehot = np.zeros((N_STN * 128, 4 * STATIONS), np.float32)
    onehot[source, target] = 1.0
    return onehot.astype(jnp.bfloat16)


ROWS = FRAMES * S_DEV


def channelize_kernel(carried, *refs):
    v_refs, tap_refs, table_ref, out_ref = refs[:RADIX], refs[RADIX : 2 * RADIX], refs[2 * RADIX], refs[2 * RADIX + 1]
    mixed, filtered, spectra, tables, arrival = refs[2 * RADIX + 2 :]
    step = pl.program_id(0)
    outputs = FRAMES - 1 if carried else FRAMES
    load = pltpu.make_async_copy(table_ref, tables, arrival)

    @pl.when(step == 0)
    def _():
        load.start()

    def rows_chunk(chunk, _):
        polar = chunk // 2
        row = pl.multiple_of(chunk % 2 * 16, 16)
        for j in range(RADIX):
            taps = [jnp.broadcast_to(tap_refs[j][k : k + 1, :], (16, 128)) for k in range(TAPS)]
            for r in range(2):
                x = [v_refs[j][f, r, polar, pl.ds(row, 16), :].astype(F32) for f in range(FRAMES)]
                for g in range(outputs):
                    if carried:
                        pairs = [(k, FRAMES + g - k) for k in range(g + 1, TAPS)]
                    else:
                        pairs = [(k, g - k) for k in range(g + 1)]
                    total = taps[pairs[0][0]] * x[pairs[0][1]]
                    for k, f in pairs[1:]:
                        total = total + taps[k] * x[f]
                    filtered[r, j, g] = total
        column = pl.multiple_of(step * 256, 256)
        for g in range(outputs):
            re = [filtered[0, j, g] for j in range(RADIX)]
            im = [filtered[1, j, g] for j in range(RADIX)]
            ar, ai = re[0] + re[2], im[0] + im[2]
            br, bi = re[0] - re[2], im[0] - im[2]
            cr, ci = re[1] + re[3], im[1] + im[3]
            dr, di = re[1] - re[3], im[1] - im[3]
            parts = (
                (ar + cr, ai + ci),
                (br + di, bi - dr),
                (ar - cr, ai - ci),
                (br - di, bi + dr),
            )
            target = pl.multiple_of(polar * ROWS + g * S_DEV + row, 16)
            for residue, (y_re, y_im) in enumerate(parts):
                mixed[residue, pl.ds(target, 16), pl.ds(column, 128)] = y_re.astype(BF16)
                mixed[residue, pl.ds(target, 16), pl.ds(column + 128, 128)] = y_im.astype(BF16)
        return 0

    lax.fori_loop(0, 2 * (S_DEV // 16), rows_chunk, 0)

    @pl.when(step == pl.num_programs(0) - 1)
    def _():
        load.wait()
        if carried:
            for residue in range(RADIX):
                for polar in range(2):
                    last = polar * ROWS + outputs * S_DEV
                    mixed[residue, last : last + S_DEV, :] = jnp.zeros((S_DEV, 2 * POINTS), BF16)
        for residue in range(RADIX):
            product = jnp.dot(mixed[residue], tables[residue], preferred_element_type=F32)
            for seg in range(2 * SEGS):
                rows = product[seg * 128 : seg * 128 + 128]
                spectra[residue, 0, seg] = rows[:, :128].T
                spectra[residue, 1, seg] = rows[:, 128:].T
        for k in range(N_STN):
            rows = [sum(SIZES[n][residue] for n in range(k)) for residue in range(RADIX)]
            for seg in range(2 * SEGS):
                for part in range(2):
                    piece = jnp.concatenate(
                        [
                            spectra[residue, part, seg, rows[residue] : rows[residue] + SIZES[k][residue]]
                            for residue in range(RADIX)
                        ],
                        0,
                    )
                    at = slice(part * LOCAL_CHAN, (part + 1) * LOCAL_CHAN)
                    out_ref[k, seg, at] = piece.astype(out_ref.dtype)


BLOCKS = (N_STN, 2 * SEGS, 2 * LOCAL_CHAN, 128)


def channelize(voltages, taps, table, carried):
    steps = POINTS // 128
    v_specs = [
        pl.BlockSpec((FRAMES, 2, 2, S_DEV, 128), functools.partial(lambda j, i: (0, 0, 0, 0, j * steps + i), j))
        for j in range(RADIX)
    ]
    t_specs = [
        pl.BlockSpec((TAPS, 128), functools.partial(lambda j, i: (0, j * steps + i), j)) for j in range(RADIX)
    ]
    voltages, taps, table = (pltpu.with_memory_space_constraint(x, pltpu.HBM) for x in (voltages, taps, table))
    return pl.pallas_call(
        functools.partial(channelize_kernel, carried),
        out_shape=jax.ShapeDtypeStruct(BLOCKS, BF16 if carried else F32),
        grid=(steps,),
        in_specs=v_specs + t_specs + [pl.BlockSpec(memory_space=pl.ANY)],
        out_specs=pl.BlockSpec(memory_space=pltpu.VMEM),
        scratch_shapes=[
            pltpu.VMEM((RADIX, 2 * ROWS, 2 * POINTS), BF16),
            pltpu.VMEM((2, RADIX, FRAMES, 16, 128), F32),
            pltpu.VMEM((RADIX, 2, 2 * SEGS, 128, 128), F32),
            pltpu.VMEM(table.shape, BF16),
            pltpu.SemaphoreType.DMA(()),
        ],
        compiler_params=pltpu.CompilerParams(
            dimension_semantics=("arbitrary",), vmem_limit_bytes=40 * 1024 * 1024
        ),
        cost_estimate=pl.CostEstimate(flops=14_000_000_000, bytes_accessed=16_000_000, transcendentals=0),
        name="carried" if carried else "own",
    )(*([voltages] * RADIX), *([taps] * RADIX), table)


def combine_kernel(me_ref, own_ref, received_ref, tol_ref, out_ref, packed_ref, spectra, leaving):
    lane = lax.broadcasted_iota(jnp.int32, (LOCAL_CHAN, 128), 1)
    for k in range(N_STN):
        packed = None
        for polar in range(2):
            first = second = None
            for seg in range(polar * SEGS, (polar + 1) * SEGS):
                value = (own_ref[k, seg] + received_ref[k, seg].astype(F32)).astype(BF16)
                spectra[k, seg] = value
                value = value.astype(F32)
                power = value[:LOCAL_CHAN] * value[:LOCAL_CHAN] + value[LOCAL_CHAN:] * value[LOCAL_CHAN:]
                square = power * power
                first = power if first is None else first + power
                second = square if second is None else second + square
            for kind, total in enumerate((first, second)):
                total = total + pltpu.roll(total, 64, 1)
                total = total + pltpu.roll(total, 32, 1)
                group = 2 * polar + kind
                packed = total if group == 0 else jnp.where(lane // 32 == group, total, packed)
        pltpu.make_async_copy(spectra.at[k], out_ref.at[k], leaving.at[k]).start()
        packed_ref[lax.rem(k + N_STN - me_ref[0], N_STN)] = packed
    packed_ref[N_STN] = tol_ref[...]
    for k in range(N_STN):
        pltpu.make_async_copy(spectra.at[k], out_ref.at[k], leaving.at[k]).wait()


def combine(me, own, received, tolerances):
    vmem = pl.BlockSpec(memory_space=pltpu.VMEM)
    return pl.pallas_call(
        combine_kernel,
        out_shape=[
            jax.ShapeDtypeStruct(BLOCKS, BF16),
            jax.ShapeDtypeStruct((N_STN + 1, LOCAL_CHAN, 128), F32),
        ],
        in_specs=[pl.BlockSpec(memory_space=pltpu.SMEM), vmem, vmem, vmem],
        out_specs=[pl.BlockSpec(memory_space=pltpu.HBM), vmem],
        scratch_shapes=[pltpu.VMEM(BLOCKS, BF16), pltpu.SemaphoreType.DMA((N_STN,))],
        compiler_params=pltpu.CompilerParams(vmem_limit_bytes=16 * 1024 * 1024),
        cost_estimate=pl.CostEstimate(flops=8_000_000, bytes_accessed=8_000_000, transcendentals=0),
        name="combine",
    )(me, own, received, tolerances)


STATION_ROWS = 64


def turn(offsets, number):
    unit = 2.0 * math.pi / 65536.0
    residue = (offsets * number) & 65535
    quadrant = (residue + 8192) >> 14
    angle = (residue - (quadrant << 14)).astype(F32) * unit
    square = angle * angle
    sine = angle * (1.0 + square * (-1.0 / 6.0 + square * (1.0 / 120.0 - square * (1.0 / 5040.0))))
    cosine = 1.0 + square * (
        -0.5 + square * (1.0 / 24.0 + square * (-1.0 / 720.0 + square * (1.0 / 40320.0)))
    )
    odd = (quadrant & 1) == 1
    real = jnp.where(odd, sine, cosine)
    imag = jnp.where(odd, cosine, sine)
    real = jnp.where(((quadrant + 1) & 2) == 2, -real, real)
    imag = jnp.where((quadrant & 2) == 2, -imag, imag)
    return real, imag


def times(a, b):
    return a[0] * b[0] - a[1] * b[1], a[0] * b[1] + a[1] * b[0]


def steering_kernel(start, me_ref, plan_ref, coords_ref, flags_ref, pointings_ref, out_ref, coarse, fine):
    me = me_ref[0]
    shape = (STATION_ROWS, STATIONS)
    station = pl.program_id(0) * STATION_ROWS + lax.broadcasted_iota(jnp.int32, shape, 0)
    mine = station == lax.broadcasted_iota(jnp.int32, shape, 1)

    def column(row):
        return jnp.sum(jnp.where(mine, row.astype(F32), 0.0), 1, keepdims=True)

    east = column(coords_ref[0:1, :]).astype(jnp.int32)
    north = column(coords_ref[1:2, :]).astype(jnp.int32)
    offsets = east * pointings_ref[0:1, :] + north * pointings_ref[1:2, :]
    single = turn(offsets, 1)
    pair = times(single, single)
    fine[0, 0], fine[0, 1] = single
    fine[1, 0], fine[1, 1] = pair
    for o in range(2, OWNED):
        fine[o, 0], fine[o, 1] = times((fine[o - 2, 0], fine[o - 2, 1]), pair)
    stride = (fine[OWNED - 1, 0], fine[OWNED - 1, 1])
    double = times(stride, stride)
    fast = times(double, double)
    gain = column((1 - flags_ref[...]).astype(F32) * (1.0 / math.sqrt(STATIONS)))
    gain = jnp.broadcast_to(gain, (STATION_ROWS, BEAMS))
    value = (gain, jnp.zeros_like(gain))
    if start:
        value = tuple(part * gain for part in turn(offsets, OWNED * start))
    for t in range(4):
        coarse[t, 0], coarse[t, 1] = value
        if t < 3:
            value = times(value, stride)
    for t in range(4, N_TM // 2):
        coarse[t, 0], coarse[t, 1] = times((coarse[t - 4, 0], coarse[t - 4, 1]), fast)

    def channels(n, _):
        for i in range(4):
            at = 4 * n + i
            c = at + (start and HALF)
            t, o = plan_ref[me, 3 * LOCAL_CHAN + c] - start, plan_ref[me, 4 * LOCAL_CHAN + c]
            real, imag = times((coarse[t, 0], coarse[t, 1]), (fine[o, 0], fine[o, 1]))
            out_ref[at, :, :BEAMS] = real.astype(BF16)
            out_ref[at, :, BEAMS:] = imag.astype(BF16)
        return 0

    lax.fori_loop(0, HALF // 4, channels, 0)


HALF = LOCAL_CHAN // 2


def steering(start, me, plans, coords, flags, pointings):
    smem = pl.BlockSpec(memory_space=pltpu.SMEM)
    vmem = pl.BlockSpec(memory_space=pltpu.VMEM)
    return pl.pallas_call(
        functools.partial(steering_kernel, start),
        out_shape=jax.ShapeDtypeStruct((HALF, STATIONS, 2 * BEAMS), BF16),
        grid=(STATIONS // STATION_ROWS,),
        in_specs=[smem, smem, vmem, vmem, vmem],
        out_specs=pl.BlockSpec((HALF, STATION_ROWS, 2 * BEAMS), lambda i: (0, i, 0)),
        scratch_shapes=[
            pltpu.VMEM((N_TM // 2, 2, STATION_ROWS, BEAMS), F32),
            pltpu.VMEM((OWNED, 2, STATION_ROWS, BEAMS), F32),
        ],
        compiler_params=pltpu.CompilerParams(
            dimension_semantics=("arbitrary",), vmem_limit_bytes=54 * 1024 * 1024
        ),
        cost_estimate=pl.CostEstimate(flops=40_000, bytes_accessed=12_600, transcendentals=0),
        name="steering",
    )(me, plans, coords, flags, pointings)


def place_stations(in_ref, polar, perm_ref, out_ref):
    for seg in range(SEGS):
        stacked = jnp.concatenate([in_ref[g, polar * SEGS + seg] for g in range(N_STN)], 1)
        moved = jnp.dot(stacked, perm_ref[...], preferred_element_type=F32)
        for part in range(2):
            rows = moved[part * LOCAL_CHAN : (part + 1) * LOCAL_CHAN]
            for f4 in range(4):
                at = ((part * 4 + f4) * SEGS + seg) * LOCAL_CHAN
                for half in range(2):
                    column = f4 * STATIONS + half * 128
                    out_ref[half, at : at + LOCAL_CHAN, :] = rows[:, column : column + 128]


PLACED = (2, 32 * LOCAL_CHAN, 128)


BLOCK = 8
CHUNKS = LOCAL_CHAN // BLOCK


def beam_kernel(me_ref, plan_ref, tol_ref, *refs):
    sum_refs = refs[:N_STN]
    in_ref, perm_ref, low_ref, high_ref, out_ref = refs[N_STN : N_STN + 5]
    window_sums, ordered, first_placed, second_placed, perm, weights, powers, arrival = refs[N_STN + 5 :]

    def load(chunk):
        source, at = (low_ref, chunk) if chunk < CHUNKS // 2 else (high_ref, chunk - CHUNKS // 2)
        return pltpu.make_async_copy(
            source.at[pl.ds(at * BLOCK, BLOCK)], weights.at[pl.ds(chunk * BLOCK, BLOCK)], arrival.at[chunk]
        )

    load_perm = pltpu.make_async_copy(perm_ref, perm, arrival.at[CHUNKS])
    load_perm.start()
    for chunk in range(CHUNKS):
        load(chunk).start()
    powers[...] = jnp.zeros_like(powers)
    lane = lax.broadcasted_iota(jnp.int32, (LOCAL_CHAN, 128), 1)
    for d in range(N_STN):
        ordered[lax.rem(me_ref[0] + N_STN - d, N_STN)] = sum_refs[d][...]
    for polar in range(2):
        for kind in range(2):
            group = 2 * polar + kind
            for half in range(2):
                total = jnp.zeros((LOCAL_CHAN, 128), F32)
                for place in range(4):
                    shift = 32 * ((place - group) % 4)
                    piece = ordered[4 * half + place]
                    if shift:
                        piece = pltpu.roll(piece, shift, 1)
                    total = jnp.where(lane // 32 == place, piece, total)
                window_sums[polar, kind, :, half * 128 : half * 128 + 128] = total
    load_perm.wait()
    place_stations(in_ref, 0, perm, first_placed)
    place_stations(in_ref, 1, perm, second_placed)

    size = float(WINDOW * FRAMES)

    for chunk in range(CHUNKS):
        load(chunk).wait()
        for inner in range(BLOCK):
            visit = chunk * BLOCK + inner
            local = plan_ref[me_ref[0], 2 * LOCAL_CHAN + visit]
            tolerance = tol_ref[plan_ref[me_ref[0], visit]]
            rows = []
            for polar, ref in enumerate((first_placed, second_placed)):
                s1 = window_sums[polar, 0, pl.ds(local, 1), :]
                s2 = window_sums[polar, 1, pl.ds(local, 1), :]
                kurtosis = (size + 1.0) / (size - 1.0) * (size * s2 / (s1 * s1) - 1.0)
                deviation = (kurtosis - 1.0) / tolerance
                soft = 1.0 / (1.0 + deviation * deviation)
                halves = [ref[half, pl.ds(local, 32, stride=LOCAL_CHAN), :] for half in range(2)]
                values = jnp.concatenate(halves, 1)
                rows.append((values * soft).astype(BF16))
            stacked = jnp.concatenate([rows[0][:16], rows[1][:16], rows[0][16:], rows[1][16:]], 0)
            product = jnp.dot(stacked, weights[visit], preferred_element_type=F32)
            real = product[:32, :BEAMS] - product[32:, BEAMS:]
            imag = product[:32, BEAMS:] + product[32:, :BEAMS]
            power = jnp.sum(real * real + imag * imag, 0, keepdims=True) * (1.0 / (2.0 * INTEG))
            powers[pl.ds(plan_ref[me_ref[0], LOCAL_CHAN + visit], 1), :] = power

    share = BEAMS // N_STN
    out_ref[...] = jnp.zeros_like(out_ref)
    for slot in range(2):
        rows = powers[slot * N_TM : (slot + 1) * N_TM, :]
        for j in range(N_STN):
            out_ref[:, j, slot * share : (slot + 1) * share] = rows[:, j * share : (j + 1) * share]


def beams(me, plans, tolerance, sums, arrived, perm, low, high):
    smem = pl.BlockSpec(memory_space=pltpu.SMEM)
    vmem = pl.BlockSpec(memory_space=pltpu.VMEM)
    low, high, perm = (pltpu.with_memory_space_constraint(x, pltpu.HBM) for x in (low, high, perm))
    return pl.pallas_call(
        beam_kernel,
        out_shape=jax.ShapeDtypeStruct((N_TM, N_STN, 128), F32),
        in_specs=[smem] * 3 + [vmem] * (N_STN + 1) + [pl.BlockSpec(memory_space=pl.ANY)] * 3,
        out_specs=vmem,
        scratch_shapes=[
            pltpu.VMEM((2, 2, LOCAL_CHAN, STATIONS), F32),
            pltpu.VMEM((N_STN, LOCAL_CHAN, 128), F32),
            pltpu.VMEM(PLACED, F32),
            pltpu.VMEM(PLACED, F32),
            pltpu.VMEM(perm.shape, BF16),
            pltpu.VMEM((LOCAL_CHAN, STATIONS, 2 * BEAMS), BF16),
            pltpu.VMEM((2 * N_TM, BEAMS), F32),
            pltpu.SemaphoreType.DMA((CHUNKS + 1,)),
        ],
        compiler_params=pltpu.CompilerParams(vmem_limit_bytes=36 * 1024 * 1024),
        cost_estimate=pl.CostEstimate(flops=2_400_000_000, bytes_accessed=16_000_000, transcendentals=0),
        name="beams",
    )(me, plans, tolerance, *sums, arrived, perm, low, high)


def settle_kernel(t_ref, in_ref, out_ref):
    for offset in range(OWNED):
        group = EVEN if offset in EVEN else ODD
        parity = 0 if offset in EVEN else 1
        k = 2 * lax.rem(group.index(offset) + t_ref[0], 4) + parity
        column = slot_of(offset) * 32
        out_ref[offset] = in_ref[pl.ds(k, N_TM, stride=N_STN), :][:, column : column + 32]


def settle(t, arrived):
    vmem = pl.BlockSpec(memory_space=pltpu.VMEM)
    return pl.pallas_call(
        settle_kernel,
        out_shape=jax.ShapeDtypeStruct((OWNED, N_TM, BEAMS // N_STN), F32),
        in_specs=[pl.BlockSpec(memory_space=pltpu.SMEM), vmem],
        out_specs=vmem,
        name="settle",
    )(t, arrived)


def across_stations(blocks):
    return lax.all_to_all(blocks, "stn", split_axis=0, concat_axis=0, tiled=True)


def after(value, *others):
    return lax.optimization_barrier((value, *others))[0]


def permuted(block, axis, send_to):
    return lax.ppermute(block, axis, [(i, send_to(i)) for i in range(lax.axis_size(axis))])


def window_round(sums, bits):
    parts = [permuted(sums, "tm", lambda i, flip=flip: i ^ flip) for flip in (bits[0], bits[1], bits[0] | bits[1])]
    return (sums + parts[0]) + (parts[1] + parts[2])


def per_device(voltages, taps, sk_tolerance, station_coords, pointings, station_flags):
    stn = lax.axis_index("stn")
    tm = lax.axis_index("tm")
    me = jnp.reshape(stn, (1,)).astype(jnp.int32)
    table = jnp.asarray(dft_tables())
    perm = jnp.asarray(lane_permutation())
    shift = [(i, i + 1) for i in range(N_TM - 1)]

    visited = np.array(VISITED)
    plans = np.stack([visited, np.array(VISITED_SLOTS), np.array(ORDER), visited // OWNED, visited % OWNED], 1)
    plans = jnp.asarray(plans.astype(np.int32).reshape(N_STN, 5 * LOCAL_CHAN))
    geometry = (station_coords.T, station_flags[None, :], pointings.T)

    leaving = channelize(voltages, taps, table, True)
    received = lax.ppermute(leaving, "tm", shift)
    holder = jnp.arange(CHAN, dtype=jnp.int32) // OWNED
    tolerances = jnp.where(holder == tm, jnp.tile(sk_tolerance, N_TM), 0.0)
    tolerances = jnp.pad(tolerances.reshape(CHAN // 128, 128), ((0, LOCAL_CHAN - CHAN // 128), (0, 0)))

    own = channelize(after(voltages, leaving), taps, table, False)
    blocks, sums = combine(me, own, received, tolerances)
    arrived = across_stations(blocks)
    sums = window_round(sums, (1, 2))
    low = steering(0, after(me, blocks), plans, *geometry)
    sums = window_round(after(sums, low), (4, 8))
    high = steering(N_TM // 2, after(me, low), plans, *geometry)
    sums = after(sums, high)
    tolerance = sums[N_STN, :8]
    tolerance = tolerance + permuted(tolerance, "tm", lambda i: i ^ WINDOW)
    tolerance = tolerance[: CHAN // 128].reshape(CHAN)
    window = [sums[0]] + [
        permuted(sums[d], "stn", lambda i, d=d: (i + d) % N_STN) for d in range(1, N_STN)
    ]
    outgoing = beams(me, plans, tolerance, window, arrived, perm, low, high)
    outgoing = outgoing.reshape(N_TM * N_STN, 1, 128)
    landed = lax.all_to_all(outgoing, ("tm", "stn"), split_axis=0, concat_axis=0, tiled=True)
    return settle(jnp.reshape(tm, (1,)).astype(jnp.int32), landed.reshape(N_TM * N_STN, 128))


def solution(mesh):
    in_specs = (P("tm", None, None, "stn", None), P(), P("tm"), P(), P(), P())
    out_specs = P("tm", None, "stn")
    return jax.shard_map(
        per_device, mesh=mesh, in_specs=in_specs, out_specs=out_specs, check_vma=False
    )
```

```python
import functools
import math

import jax
import jax.numpy as jnp
import numpy as np
from jax import lax
from jax.experimental import pallas as pl
from jax.experimental.pallas import tpu as pltpu
from jax.sharding import PartitionSpec as P

STATIONS = 256
NFFT = 2048
CHAN = 384
BEAMS = 256
INTEG = 16
TAPS = 16
FRAMES = 16
N_STN = 8
N_TM = 32
S_DEV = 32
LOCAL_CHAN = CHAN // N_STN
OWNED = CHAN // N_TM
WINDOW = 16
RADIX = 4
POINTS = NFFT // RADIX
SEGS = 4
F32 = jnp.float32
BF16 = jnp.bfloat16

EVEN = (0, 4, 1, 5, 10, 11)
ODD = (2, 6, 3, 7, 8, 9)


def stn_of(offset, t):
    if offset in EVEN:
        return 2 * ((EVEN.index(offset) + t) % 4)
    return 2 * ((ODD.index(offset) + t) % 4) + 1


def slot_of(offset):
    return 1 if offset >= 8 else 0


def channel_plan():
    channels, slots, sizes = [], [], []
    for k in range(N_STN):
        mine, places, count = [], [], []
        for residue in range(RADIX):
            before = len(mine)
            for t in range(N_TM):
                for offset in range(residue, OWNED, RADIX):
                    if stn_of(offset, t) == k:
                        mine.append(OWNED * t + offset)
                        places.append(N_TM * slot_of(offset) + t)
            count.append(len(mine) - before)
        assert len(mine) == LOCAL_CHAN and len(set(places)) == LOCAL_CHAN
        assert all(n % 8 == 0 for n in count)
        channels.append(mine)
        slots.append(places)
        sizes.append(count)
    return channels, slots, sizes


CHANNELS, SLOTS, SIZES = channel_plan()
ORDER = [sorted(range(LOCAL_CHAN), key=lambda n, mine=mine: mine[n]) for mine in CHANNELS]
VISITED = [[mine[n] for n in order] for mine, order in zip(CHANNELS, ORDER)]
assert all(c // OWNED // (N_TM // 2) == n // (LOCAL_CHAN // 2) for mine in VISITED for n, c in enumerate(mine))
VISITED_SLOTS = [[places[n] for n in order] for places, order in zip(SLOTS, ORDER)]


def dft_tables():
    tables = []
    points = np.arange(POINTS)
    for residue in range(RADIX):
        order = []
        for k in range(N_STN):
            start = sum(SIZES[k][:residue])
            order += CHANNELS[k][start : start + SIZES[k][residue]]
        turns = (np.array(order)[:, None] * points[None, :]) % NFFT
        angle = 2.0 * np.pi * turns / NFFT
        cosine = np.cos(angle) / math.sqrt(NFFT)
        sine = np.sin(angle) / math.sqrt(NFFT)
        real_rows = np.stack([cosine, sine], 1)
        imag_rows = np.stack([-sine, cosine], 1)
        columns = np.zeros((2 * POINTS, 256))
        for part, rows in enumerate((real_rows, imag_rows)):
            rows = rows.reshape(-1, 2, POINTS // 128, 128).transpose(2, 1, 3, 0)
            columns[:, 128 * part : 128 * part + CHAN // RADIX] = rows.reshape(2 * POINTS, -1)
        tables.append(columns)
    return np.stack(tables, 0).astype(np.float32).astype(jnp.bfloat16)


def lane_permutation():
    source = np.arange(N_STN * 128)
    d, f4, s = source // 128, source // 32 % 4, source % 32
    target = f4 * STATIONS + d * S_DEV + s
    onehot = np.zeros((N_STN * 128, 4 * STATIONS), np.float32)
    onehot[source, target] = 1.0
    return onehot.astype(jnp.bfloat16)


ROWS = FRAMES * S_DEV


def channelize_kernel(carried, *refs):
    v_refs, tap_refs, table_ref, out_ref = refs[:RADIX], refs[RADIX : 2 * RADIX], refs[2 * RADIX], refs[2 * RADIX + 1]
    mixed, filtered, spectra, tables, arrival = refs[2 * RADIX + 2 :]
    step = pl.program_id(0)
    outputs = FRAMES - 1 if carried else FRAMES
    load = pltpu.make_async_copy(table_ref, tables, arrival)

    @pl.when(step == 0)
    def _():
        load.start()

    def rows_chunk(chunk, _):
        polar = chunk // 2
        row = pl.multiple_of(chunk % 2 * 16, 16)
        for j in range(RADIX):
            taps = [jnp.broadcast_to(tap_refs[j][k : k + 1, :], (16, 128)) for k in range(TAPS)]
            for r in range(2):
                x = [v_refs[j][f, r, polar, pl.ds(row, 16), :].astype(F32) for f in range(FRAMES)]
                for g in range(outputs):
                    if carried:
                        pairs = [(k, FRAMES + g - k) for k in range(g + 1, TAPS)]
                    else:
                        pairs = [(k, g - k) for k in range(g + 1)]
                    total = taps[pairs[0][0]] * x[pairs[0][1]]
                    for k, f in pairs[1:]:
                        total = total + taps[k] * x[f]
                    filtered[r, j, g] = total
        column = pl.multiple_of(step * 256, 256)
        for g in range(outputs):
            re = [filtered[0, j, g] for j in range(RADIX)]
            im = [filtered[1, j, g] for j in range(RADIX)]
            ar, ai = re[0] + re[2], im[0] + im[2]
            br, bi = re[0] - re[2], im[0] - im[2]
            cr, ci = re[1] + re[3], im[1] + im[3]
            dr, di = re[1] - re[3], im[1] - im[3]
            parts = (
                (ar + cr, ai + ci),
                (br + di, bi - dr),
                (ar - cr, ai - ci),
                (br - di, bi + dr),
            )
            target = pl.multiple_of(polar * ROWS + g * S_DEV + row, 16)
            for residue, (y_re, y_im) in enumerate(parts):
                mixed[residue, pl.ds(target, 16), pl.ds(column, 128)] = y_re.astype(BF16)
                mixed[residue, pl.ds(target, 16), pl.ds(column + 128, 128)] = y_im.astype(BF16)
        return 0

    lax.fori_loop(0, 2 * (S_DEV // 16), rows_chunk, 0)

    @pl.when(step == pl.num_programs(0) - 1)
    def _():
        load.wait()
        if carried:
            for residue in range(RADIX):
                for polar in range(2):
                    last = polar * ROWS + outputs * S_DEV
                    mixed[residue, last : last + S_DEV, :] = jnp.zeros((S_DEV, 2 * POINTS), BF16)
        for residue in range(RADIX):
            product = jnp.dot(mixed[residue], tables[residue], preferred_element_type=F32)
            for seg in range(2 * SEGS):
                rows = product[seg * 128 : seg * 128 + 128]
                spectra[residue, 0, seg] = rows[:, :128].T
                spectra[residue, 1, seg] = rows[:, 128:].T
        for k in range(N_STN):
            rows = [sum(SIZES[n][residue] for n in range(k)) for residue in range(RADIX)]
            for seg in range(2 * SEGS):
                for part in range(2):
                    piece = jnp.concatenate(
                        [
                            spectra[residue, part, seg, rows[residue] : rows[residue] + SIZES[k][residue]]
                            for residue in range(RADIX)
                        ],
                        0,
                    )
                    at = slice(part * LOCAL_CHAN, (part + 1) * LOCAL_CHAN)
                    out_ref[k, seg, at] = piece.astype(out_ref.dtype)


BLOCKS = (N_STN, 2 * SEGS, 2 * LOCAL_CHAN, 128)


def channelize(voltages, taps, table, carried):
    steps = POINTS // 128
    v_specs = [
        pl.BlockSpec((FRAMES, 2, 2, S_DEV, 128), functools.partial(lambda j, i: (0, 0, 0, 0, j * steps + i), j))
        for j in range(RADIX)
    ]
    t_specs = [
        pl.BlockSpec((TAPS, 128), functools.partial(lambda j, i: (0, j * steps + i), j)) for j in range(RADIX)
    ]
    voltages, taps, table = (pltpu.with_memory_space_constraint(x, pltpu.HBM) for x in (voltages, taps, table))
    return pl.pallas_call(
        functools.partial(channelize_kernel, carried),
        out_shape=jax.ShapeDtypeStruct(BLOCKS, BF16 if carried else F32),
        grid=(steps,),
        in_specs=v_specs + t_specs + [pl.BlockSpec(memory_space=pl.ANY)],
        out_specs=pl.BlockSpec(memory_space=pltpu.VMEM),
        scratch_shapes=[
            pltpu.VMEM((RADIX, 2 * ROWS, 2 * POINTS), BF16),
            pltpu.VMEM((2, RADIX, FRAMES, 16, 128), F32),
            pltpu.VMEM((RADIX, 2, 2 * SEGS, 128, 128), F32),
            pltpu.VMEM(table.shape, BF16),
            pltpu.SemaphoreType.DMA(()),
        ],
        compiler_params=pltpu.CompilerParams(
            dimension_semantics=("arbitrary",), vmem_limit_bytes=40 * 1024 * 1024
        ),
        cost_estimate=pl.CostEstimate(flops=14_000_000_000, bytes_accessed=16_000_000, transcendentals=0),
        name="carried" if carried else "own",
    )(*([voltages] * RADIX), *([taps] * RADIX), table)


def combine_kernel(me_ref, own_ref, received_ref, tol_ref, out_ref, packed_ref, spectra, leaving):
    lane = lax.broadcasted_iota(jnp.int32, (LOCAL_CHAN, 128), 1)
    for k in range(N_STN):
        packed = None
        for polar in range(2):
            first = second = None
            for seg in range(polar * SEGS, (polar + 1) * SEGS):
                value = (own_ref[k, seg] + received_ref[k, seg].astype(F32)).astype(BF16)
                spectra[k, seg] = value
                value = value.astype(F32)
                power = value[:LOCAL_CHAN] * value[:LOCAL_CHAN] + value[LOCAL_CHAN:] * value[LOCAL_CHAN:]
                square = power * power
                first = power if first is None else first + power
                second = square if second is None else second + square
            for kind, total in enumerate((first, second)):
                total = total + pltpu.roll(total, 64, 1)
                total = total + pltpu.roll(total, 32, 1)
                group = 2 * polar + kind
                packed = total if group == 0 else jnp.where(lane // 32 == group, total, packed)
        pltpu.make_async_copy(spectra.at[k], out_ref.at[k], leaving.at[k]).start()
        packed_ref[lax.rem(k + N_STN - me_ref[0], N_STN)] = packed
    packed_ref[N_STN] = tol_ref[...]
    for k in range(N_STN):
        pltpu.make_async_copy(spectra.at[k], out_ref.at[k], leaving.at[k]).wait()


def combine(me, own, received, tolerances):
    vmem = pl.BlockSpec(memory_space=pltpu.VMEM)
    return pl.pallas_call(
        combine_kernel,
        out_shape=[
            jax.ShapeDtypeStruct(BLOCKS, BF16),
            jax.ShapeDtypeStruct((N_STN + 1, LOCAL_CHAN, 128), F32),
        ],
        in_specs=[pl.BlockSpec(memory_space=pltpu.SMEM), vmem, vmem, vmem],
        out_specs=[pl.BlockSpec(memory_space=pltpu.HBM), vmem],
        scratch_shapes=[pltpu.VMEM(BLOCKS, BF16), pltpu.SemaphoreType.DMA((N_STN,))],
        compiler_params=pltpu.CompilerParams(vmem_limit_bytes=16 * 1024 * 1024),
        cost_estimate=pl.CostEstimate(flops=8_000_000, bytes_accessed=8_000_000, transcendentals=0),
        name="combine",
    )(me, own, received, tolerances)


STATION_ROWS = 64


def turn(offsets, number):
    unit = 2.0 * math.pi / 65536.0
    residue = (offsets * number) & 65535
    quadrant = (residue + 8192) >> 14
    angle = (residue - (quadrant << 14)).astype(F32) * unit
    square = angle * angle
    sine = angle * (1.0 + square * (-1.0 / 6.0 + square * (1.0 / 120.0 - square * (1.0 / 5040.0))))
    cosine = 1.0 + square * (
        -0.5 + square * (1.0 / 24.0 + square * (-1.0 / 720.0 + square * (1.0 / 40320.0)))
    )
    odd = (quadrant & 1) == 1
    real = jnp.where(odd, sine, cosine)
    imag = jnp.where(odd, cosine, sine)
    real = jnp.where(((quadrant + 1) & 2) == 2, -real, real)
    imag = jnp.where((quadrant & 2) == 2, -imag, imag)
    return real, imag


def times(a, b):
    return a[0] * b[0] - a[1] * b[1], a[0] * b[1] + a[1] * b[0]


def steering_kernel(start, me_ref, plan_ref, coords_ref, flags_ref, pointings_ref, out_ref, coarse, fine):
    me = me_ref[0]
    shape = (STATION_ROWS, STATIONS)
    station = pl.program_id(0) * STATION_ROWS + lax.broadcasted_iota(jnp.int32, shape, 0)
    mine = station == lax.broadcasted_iota(jnp.int32, shape, 1)

    def column(row):
        return jnp.sum(jnp.where(mine, row.astype(F32), 0.0), 1, keepdims=True)

    east = column(coords_ref[0:1, :]).astype(jnp.int32)
    north = column(coords_ref[1:2, :]).astype(jnp.int32)
    offsets = east * pointings_ref[0:1, :] + north * pointings_ref[1:2, :]
    single = turn(offsets, 1)
    pair = times(single, single)
    fine[0, 0], fine[0, 1] = single
    fine[1, 0], fine[1, 1] = pair
    for o in range(2, OWNED):
        fine[o, 0], fine[o, 1] = times((fine[o - 2, 0], fine[o - 2, 1]), pair)
    stride = (fine[OWNED - 1, 0], fine[OWNED - 1, 1])
    double = times(stride, stride)
    fast = times(double, double)
    gain = column((1 - flags_ref[...]).astype(F32) * (1.0 / math.sqrt(STATIONS)))
    gain = jnp.broadcast_to(gain, (STATION_ROWS, BEAMS))
    value = (gain, jnp.zeros_like(gain))
    if start:
        value = tuple(part * gain for part in turn(offsets, OWNED * start))
    for t in range(4):
        coarse[t, 0], coarse[t, 1] = value
        if t < 3:
            value = times(value, stride)
    for t in range(4, N_TM // 2):
        coarse[t, 0], coarse[t, 1] = times((coarse[t - 4, 0], coarse[t - 4, 1]), fast)

    def channels(n, _):
        for i in range(4):
            at = 4 * n + i
            c = at + (start and HALF)
            t, o = plan_ref[me, 3 * LOCAL_CHAN + c] - start, plan_ref[me, 4 * LOCAL_CHAN + c]
            real, imag = times((coarse[t, 0], coarse[t, 1]), (fine[o, 0], fine[o, 1]))
            out_ref[at, :, :BEAMS] = real.astype(BF16)
            out_ref[at, :, BEAMS:] = imag.astype(BF16)
        return 0

    lax.fori_loop(0, HALF // 4, channels, 0)


HALF = LOCAL_CHAN // 2


def steering(start, me, plans, coords, flags, pointings):
    smem = pl.BlockSpec(memory_space=pltpu.SMEM)
    vmem = pl.BlockSpec(memory_space=pltpu.VMEM)
    return pl.pallas_call(
        functools.partial(steering_kernel, start),
        out_shape=jax.ShapeDtypeStruct((HALF, STATIONS, 2 * BEAMS), BF16),
        grid=(STATIONS // STATION_ROWS,),
        in_specs=[smem, smem, vmem, vmem, vmem],
        out_specs=pl.BlockSpec((HALF, STATION_ROWS, 2 * BEAMS), lambda i: (0, i, 0)),
        scratch_shapes=[
            pltpu.VMEM((N_TM // 2, 2, STATION_ROWS, BEAMS), F32),
            pltpu.VMEM((OWNED, 2, STATION_ROWS, BEAMS), F32),
        ],
        compiler_params=pltpu.CompilerParams(
            dimension_semantics=("arbitrary",), vmem_limit_bytes=54 * 1024 * 1024
        ),
        cost_estimate=pl.CostEstimate(flops=40_000, bytes_accessed=12_600, transcendentals=0),
        name="steering",
    )(me, plans, coords, flags, pointings)


def place_stations(in_ref, polar, perm_ref, out_ref):
    rows = SEGS * 2 * LOCAL_CHAN
    own = slice(polar * SEGS, (polar + 1) * SEGS)
    stacked = jnp.concatenate([in_ref[g, own].reshape(rows, 128) for g in range(N_STN)], 1)
    for f4 in range(4):
        columns = slice(f4 * STATIONS, (f4 + 1) * STATIONS)
        moved = jnp.dot(stacked, perm_ref[:, columns], preferred_element_type=F32)
        for seg in range(SEGS):
            for part in range(2):
                source = (seg * 2 + part) * LOCAL_CHAN
                at = ((part * 4 + f4) * SEGS + seg) * LOCAL_CHAN
                for half in range(2):
                    piece = moved[source : source + LOCAL_CHAN, half * 128 : half * 128 + 128]
                    out_ref[half, at : at + LOCAL_CHAN, :] = piece


PLACED = (2, 32 * LOCAL_CHAN, 128)


BLOCK = 8
CHUNKS = LOCAL_CHAN // BLOCK


def beam_kernel(me_ref, plan_ref, tol_ref, *refs):
    sum_refs = refs[:N_STN]
    in_ref, perm_ref, low_ref, high_ref, out_ref = refs[N_STN : N_STN + 5]
    window_sums, ordered, first_placed, second_placed, perm, weights, powers, tolerances, softs, arrival = refs[N_STN + 5 :]

    def load(chunk):
        source, at = (low_ref, chunk) if chunk < CHUNKS // 2 else (high_ref, chunk - CHUNKS // 2)
        return pltpu.make_async_copy(
            source.at[pl.ds(at * BLOCK, BLOCK)], weights.at[pl.ds(chunk * BLOCK, BLOCK)], arrival.at[chunk]
        )

    load_perm = pltpu.make_async_copy(perm_ref, perm, arrival.at[CHUNKS])
    load_perm.start()
    for chunk in range(CHUNKS):
        load(chunk).start()
    load_perm.wait()
    place_stations(in_ref, 0, perm, first_placed)
    place_stations(in_ref, 1, perm, second_placed)
    powers[...] = jnp.zeros_like(powers)
    lane = lax.broadcasted_iota(jnp.int32, (LOCAL_CHAN, 128), 1)
    for d in range(N_STN):
        ordered[lax.rem(me_ref[0] + N_STN - d, N_STN)] = sum_refs[d][...]
    for polar in range(2):
        for kind in range(2):
            group = 2 * polar + kind
            for half in range(2):
                total = jnp.zeros((LOCAL_CHAN, 128), F32)
                for place in range(4):
                    shift = 32 * ((place - group) % 4)
                    piece = ordered[4 * half + place]
                    if shift:
                        piece = pltpu.roll(piece, shift, 1)
                    total = jnp.where(lane // 32 == place, piece, total)
                window_sums[polar, kind, :, half * 128 : half * 128 + 128] = total
    for visit in range(LOCAL_CHAN):
        tolerance = tol_ref[plan_ref[me_ref[0], visit]]
        row = pl.ds(plan_ref[me_ref[0], 2 * LOCAL_CHAN + visit], 1)
        tolerances[row, :] = jnp.full((1, STATIONS), tolerance, F32)
    size = float(WINDOW * FRAMES)
    for polar in range(2):
        s1, s2 = window_sums[polar, 0], window_sums[polar, 1]
        kurtosis = (size + 1.0) / (size - 1.0) * (size * s2 / (s1 * s1) - 1.0)
        deviation = (kurtosis - 1.0) / tolerances[...]
        softs[polar] = 1.0 / (1.0 + deviation * deviation)

    for chunk in range(CHUNKS):
        load(chunk).wait()
        for inner in range(BLOCK):
            visit = chunk * BLOCK + inner
            local = plan_ref[me_ref[0], 2 * LOCAL_CHAN + visit]
            rows = []
            for polar, ref in enumerate((first_placed, second_placed)):
                soft = softs[polar, pl.ds(local, 1), :]
                halves = [ref[half, pl.ds(local, 32, stride=LOCAL_CHAN), :] for half in range(2)]
                values = jnp.concatenate(halves, 1)
                rows.append((values * soft).astype(BF16))
            stacked = jnp.concatenate([rows[0][:16], rows[1][:16], rows[0][16:], rows[1][16:]], 0)
            product = jnp.dot(stacked, weights[visit], preferred_element_type=F32)
            real = product[:32, :BEAMS] - product[32:, BEAMS:]
            imag = product[:32, BEAMS:] + product[32:, :BEAMS]
            power = jnp.sum(real * real + imag * imag, 0, keepdims=True) * (1.0 / (2.0 * INTEG))
            powers[pl.ds(plan_ref[me_ref[0], LOCAL_CHAN + visit], 1), :] = power

    share = BEAMS // N_STN
    out_ref[...] = jnp.zeros_like(out_ref)
    for slot in range(2):
        rows = powers[slot * N_TM : (slot + 1) * N_TM, :]
        for j in range(N_STN):
            out_ref[:, j, slot * share : (slot + 1) * share] = rows[:, j * share : (j + 1) * share]


def beams(me, plans, tolerance, sums, arrived, perm, low, high):
    smem = pl.BlockSpec(memory_space=pltpu.SMEM)
    vmem = pl.BlockSpec(memory_space=pltpu.VMEM)
    low, high, perm = (pltpu.with_memory_space_constraint(x, pltpu.HBM) for x in (low, high, perm))
    return pl.pallas_call(
        beam_kernel,
        out_shape=jax.ShapeDtypeStruct((N_TM, N_STN, 128), F32),
        in_specs=[smem] * 3 + [vmem] * (N_STN + 1) + [pl.BlockSpec(memory_space=pl.ANY)] * 3,
        out_specs=vmem,
        scratch_shapes=[
            pltpu.VMEM((2, 2, LOCAL_CHAN, STATIONS), F32),
            pltpu.VMEM((N_STN, LOCAL_CHAN, 128), F32),
            pltpu.VMEM(PLACED, F32),
            pltpu.VMEM(PLACED, F32),
            pltpu.VMEM(perm.shape, BF16),
            pltpu.VMEM((LOCAL_CHAN, STATIONS, 2 * BEAMS), BF16),
            pltpu.VMEM((2 * N_TM, BEAMS), F32),
            pltpu.VMEM((LOCAL_CHAN, STATIONS), F32),
            pltpu.VMEM((2, LOCAL_CHAN, STATIONS), F32),
            pltpu.SemaphoreType.DMA((CHUNKS + 1,)),
        ],
        compiler_params=pltpu.CompilerParams(vmem_limit_bytes=36 * 1024 * 1024),
        cost_estimate=pl.CostEstimate(flops=2_400_000_000, bytes_accessed=16_000_000, transcendentals=0),
        name="beams",
    )(me, plans, tolerance, *sums, arrived, perm, low, high)


def settle_kernel(t_ref, in_ref, out_ref):
    for offset in range(OWNED):
        group = EVEN if offset in EVEN else ODD
        parity = 0 if offset in EVEN else 1
        k = 2 * lax.rem(group.index(offset) + t_ref[0], 4) + parity
        column = slot_of(offset) * 32
        out_ref[offset] = in_ref[pl.ds(k, N_TM, stride=N_STN), :][:, column : column + 32]


def settle(t, arrived):
    vmem = pl.BlockSpec(memory_space=pltpu.VMEM)
    return pl.pallas_call(
        settle_kernel,
        out_shape=jax.ShapeDtypeStruct((OWNED, N_TM, BEAMS // N_STN), F32),
        in_specs=[pl.BlockSpec(memory_space=pltpu.SMEM), vmem],
        out_specs=vmem,
        name="settle",
    )(t, arrived)


def across_stations(blocks):
    return lax.all_to_all(blocks, "stn", split_axis=0, concat_axis=0, tiled=True)


def after(value, *others):
    return lax.optimization_barrier((value, *others))[0]


def permuted(block, axis, send_to):
    return lax.ppermute(block, axis, [(i, send_to(i)) for i in range(lax.axis_size(axis))])


def window_round(sums, bits):
    parts = [permuted(sums, "tm", lambda i, flip=flip: i ^ flip) for flip in (bits[0], bits[1], bits[0] | bits[1])]
    return (sums + parts[0]) + (parts[1] + parts[2])


def per_device(voltages, taps, sk_tolerance, station_coords, pointings, station_flags):
    stn = lax.axis_index("stn")
    tm = lax.axis_index("tm")
    me = jnp.reshape(stn, (1,)).astype(jnp.int32)
    table = jnp.asarray(dft_tables())
    perm = jnp.asarray(lane_permutation())
    shift = [(i, i + 1) for i in range(N_TM - 1)]

    visited = np.array(VISITED)
    plans = np.stack([visited, np.array(VISITED_SLOTS), np.array(ORDER), visited // OWNED, visited % OWNED], 1)
    plans = jnp.asarray(plans.astype(np.int32).reshape(N_STN, 5 * LOCAL_CHAN))
    geometry = (station_coords.T, station_flags[None, :], pointings.T)

    leaving = channelize(voltages, taps, table, True)
    received = lax.ppermute(leaving, "tm", shift)
    holder = jnp.arange(CHAN, dtype=jnp.int32) // OWNED
    tolerances = jnp.where(holder == tm, jnp.tile(sk_tolerance, N_TM), 0.0)
    tolerances = jnp.pad(tolerances.reshape(CHAN // 128, 128), ((0, LOCAL_CHAN - CHAN // 128), (0, 0)))

    own = channelize(after(voltages, leaving), taps, table, False)
    blocks, sums = combine(me, own, received, tolerances)
    arrived = across_stations(blocks)
    sums = window_round(sums, (1, 2))
    low = steering(0, after(me, blocks), plans, *geometry)
    sums = window_round(after(sums, low), (4, 8))
    high = steering(N_TM // 2, after(me, low), plans, *geometry)
    sums = after(sums, high)
    tolerance = sums[N_STN, :8]
    tolerance = tolerance + permuted(tolerance, "tm", lambda i: i ^ WINDOW)
    tolerance = tolerance[: CHAN // 128].reshape(CHAN)
    window = [sums[0]] + [
        permuted(sums[d], "stn", lambda i, d=d: (i + d) % N_STN) for d in range(1, N_STN)
    ]
    outgoing = beams(me, plans, tolerance, window, arrived, perm, low, high)
    outgoing = outgoing.reshape(N_TM * N_STN, 1, 128)
    landed = lax.all_to_all(outgoing, ("tm", "stn"), split_axis=0, concat_axis=0, tiled=True)
    return settle(jnp.reshape(tm, (1,)).astype(jnp.int32), landed.reshape(N_TM * N_STN, 128))


def solution(mesh):
    in_specs = (P("tm", None, None, "stn", None), P(), P("tm"), P(), P(), P())
    out_specs = P("tm", None, "stn")
    return jax.shard_map(
        per_device, mesh=mesh, in_specs=in_specs, out_specs=out_specs, check_vma=False
    )
```

```python
import functools
import math

import jax
import jax.numpy as jnp
import numpy as np
from jax import lax
from jax.experimental import pallas as pl
from jax.experimental.pallas import tpu as pltpu
from jax.sharding import PartitionSpec as P

STATIONS = 256
NFFT = 2048
CHAN = 384
BEAMS = 256
INTEG = 16
TAPS = 16
FRAMES = 16
N_STN = 8
N_TM = 32
S_DEV = 32
LOCAL_CHAN = CHAN // N_STN
OWNED = CHAN // N_TM
WINDOW = 16
RADIX = 4
POINTS = NFFT // RADIX
SEGS = 4
F32 = jnp.float32
BF16 = jnp.bfloat16

EVEN = (0, 4, 1, 5, 10, 11)
ODD = (2, 6, 3, 7, 8, 9)


def stn_of(offset, t):
    if offset in EVEN:
        return 2 * ((EVEN.index(offset) + t) % 4)
    return 2 * ((ODD.index(offset) + t) % 4) + 1


def slot_of(offset):
    return 1 if offset >= 8 else 0


def channel_plan():
    channels, slots, sizes = [], [], []
    for k in range(N_STN):
        mine, places, count = [], [], []
        for residue in range(RADIX):
            before = len(mine)
            for t in range(N_TM):
                for offset in range(residue, OWNED, RADIX):
                    if stn_of(offset, t) == k:
                        mine.append(OWNED * t + offset)
                        places.append(N_TM * slot_of(offset) + t)
            count.append(len(mine) - before)
        assert len(mine) == LOCAL_CHAN and len(set(places)) == LOCAL_CHAN
        assert all(n % 8 == 0 for n in count)
        channels.append(mine)
        slots.append(places)
        sizes.append(count)
    return channels, slots, sizes


CHANNELS, SLOTS, SIZES = channel_plan()
ORDER = [sorted(range(LOCAL_CHAN), key=lambda n, mine=mine: mine[n]) for mine in CHANNELS]
VISITED = [[mine[n] for n in order] for mine, order in zip(CHANNELS, ORDER)]
assert all(c // OWNED // (N_TM // 2) == n // (LOCAL_CHAN // 2) for mine in VISITED for n, c in enumerate(mine))
VISITED_SLOTS = [[places[n] for n in order] for places, order in zip(SLOTS, ORDER)]


def dft_tables():
    tables = []
    points = np.arange(POINTS)
    for residue in range(RADIX):
        order = []
        for k in range(N_STN):
            start = sum(SIZES[k][:residue])
            order += CHANNELS[k][start : start + SIZES[k][residue]]
        turns = (np.array(order)[:, None] * points[None, :]) % NFFT
        angle = 2.0 * np.pi * turns / NFFT
        cosine = np.cos(angle) / math.sqrt(NFFT)
        sine = np.sin(angle) / math.sqrt(NFFT)
        real_rows = np.stack([cosine, sine], 1)
        imag_rows = np.stack([-sine, cosine], 1)
        columns = np.zeros((2 * POINTS, 256))
        for part, rows in enumerate((real_rows, imag_rows)):
            rows = rows.reshape(-1, 2, POINTS // 128, 128).transpose(2, 1, 3, 0)
            columns[:, 128 * part : 128 * part + CHAN // RADIX] = rows.reshape(2 * POINTS, -1)
        tables.append(columns)
    return np.stack(tables, 0).astype(np.float32).astype(jnp.bfloat16)


def lane_permutation():
    source = np.arange(N_STN * 128)
    d, f4, s = source // 128, source // 32 % 4, source % 32
    target = f4 * STATIONS + d * S_DEV + s
    onehot = np.zeros((N_STN * 128, 4 * STATIONS), np.float32)
    onehot[source, target] = 1.0
    return onehot.astype(jnp.bfloat16)


ROWS = FRAMES * S_DEV


def channelize_kernel(carried, *refs):
    v_refs, tap_refs, table_ref, out_ref = refs[:RADIX], refs[RADIX : 2 * RADIX], refs[2 * RADIX], refs[2 * RADIX + 1]
    mixed, filtered, spectra, tables, arrival = refs[2 * RADIX + 2 :]
    step = pl.program_id(0)
    outputs = FRAMES - 1 if carried else FRAMES
    load = pltpu.make_async_copy(table_ref, tables, arrival)

    @pl.when(step == 0)
    def _():
        load.start()

    def rows_chunk(chunk, _):
        polar = chunk // 2
        row = pl.multiple_of(chunk % 2 * 16, 16)
        for j in range(RADIX):
            taps = [jnp.broadcast_to(tap_refs[j][k : k + 1, :], (16, 128)) for k in range(TAPS)]
            for r in range(2):
                x = [v_refs[j][f, r, polar, pl.ds(row, 16), :].astype(F32) for f in range(FRAMES)]
                for g in range(outputs):
                    if carried:
                        pairs = [(k, FRAMES + g - k) for k in range(g + 1, TAPS)]
                    else:
                        pairs = [(k, g - k) for k in range(g + 1)]
                    total = taps[pairs[0][0]] * x[pairs[0][1]]
                    for k, f in pairs[1:]:
                        total = total + taps[k] * x[f]
                    filtered[r, j, g] = total
        column = pl.multiple_of(step * 256, 256)
        for g in range(outputs):
            re = [filtered[0, j, g] for j in range(RADIX)]
            im = [filtered[1, j, g] for j in range(RADIX)]
            ar, ai = re[0] + re[2], im[0] + im[2]
            br, bi = re[0] - re[2], im[0] - im[2]
            cr, ci = re[1] + re[3], im[1] + im[3]
            dr, di = re[1] - re[3], im[1] - im[3]
            parts = (
                (ar + cr, ai + ci),
                (br + di, bi - dr),
                (ar - cr, ai - ci),
                (br - di, bi + dr),
            )
            target = pl.multiple_of(polar * ROWS + g * S_DEV + row, 16)
            for residue, (y_re, y_im) in enumerate(parts):
                mixed[residue, pl.ds(target, 16), pl.ds(column, 128)] = y_re.astype(BF16)
                mixed[residue, pl.ds(target, 16), pl.ds(column + 128, 128)] = y_im.astype(BF16)
        return 0

    lax.fori_loop(0, 2 * (S_DEV // 16), rows_chunk, 0)

    @pl.when(step == pl.num_programs(0) - 1)
    def _():
        load.wait()
        if carried:
            for residue in range(RADIX):
                for polar in range(2):
                    last = polar * ROWS + outputs * S_DEV
                    mixed[residue, last : last + S_DEV, :] = jnp.zeros((S_DEV, 2 * POINTS), BF16)
        for residue in range(RADIX):
            product = jnp.dot(mixed[residue], tables[residue], preferred_element_type=F32)
            for seg in range(2 * SEGS):
                rows = product[seg * 128 : seg * 128 + 128]
                spectra[residue, 0, seg] = rows[:, :128].T
                spectra[residue, 1, seg] = rows[:, 128:].T
        for k in range(N_STN):
            rows = [sum(SIZES[n][residue] for n in range(k)) for residue in range(RADIX)]
            for seg in range(2 * SEGS):
                for part in range(2):
                    piece = jnp.concatenate(
                        [
                            spectra[residue, part, seg, rows[residue] : rows[residue] + SIZES[k][residue]]
                            for residue in range(RADIX)
                        ],
                        0,
                    )
                    at = slice(part * LOCAL_CHAN, (part + 1) * LOCAL_CHAN)
                    out_ref[k, seg, at] = piece.astype(out_ref.dtype)


BLOCKS = (N_STN, 2 * SEGS, 2 * LOCAL_CHAN, 128)


def channelize(voltages, taps, table, carried):
    steps = POINTS // 128
    v_specs = [
        pl.BlockSpec((FRAMES, 2, 2, S_DEV, 128), functools.partial(lambda j, i: (0, 0, 0, 0, j * steps + i), j))
        for j in range(RADIX)
    ]
    t_specs = [
        pl.BlockSpec((TAPS, 128), functools.partial(lambda j, i: (0, j * steps + i), j)) for j in range(RADIX)
    ]
    voltages, taps, table = (pltpu.with_memory_space_constraint(x, pltpu.HBM) for x in (voltages, taps, table))
    return pl.pallas_call(
        functools.partial(channelize_kernel, carried),
        out_shape=jax.ShapeDtypeStruct(BLOCKS, BF16 if carried else F32),
        grid=(steps,),
        in_specs=v_specs + t_specs + [pl.BlockSpec(memory_space=pl.ANY)],
        out_specs=pl.BlockSpec(memory_space=pltpu.VMEM),
        scratch_shapes=[
            pltpu.VMEM((RADIX, 2 * ROWS, 2 * POINTS), BF16),
            pltpu.VMEM((2, RADIX, FRAMES, 16, 128), F32),
            pltpu.VMEM((RADIX, 2, 2 * SEGS, 128, 128), F32),
            pltpu.VMEM(table.shape, BF16),
            pltpu.SemaphoreType.DMA(()),
        ],
        compiler_params=pltpu.CompilerParams(
            dimension_semantics=("arbitrary",), vmem_limit_bytes=40 * 1024 * 1024
        ),
        cost_estimate=pl.CostEstimate(flops=14_000_000_000, bytes_accessed=16_000_000, transcendentals=0),
        name="carried" if carried else "own",
    )(*([voltages] * RADIX), *([taps] * RADIX), table)


def combine_kernel(me_ref, own_ref, received_ref, tol_ref, out_ref, packed_ref, spectra, leaving):
    lane = lax.broadcasted_iota(jnp.int32, (LOCAL_CHAN, 128), 1)
    for k in range(N_STN):
        packed = None
        for polar in range(2):
            first = second = None
            for seg in range(polar * SEGS, (polar + 1) * SEGS):
                value = (own_ref[k, seg] + received_ref[k, seg].astype(F32)).astype(BF16)
                spectra[k, seg] = value
                value = value.astype(F32)
                power = value[:LOCAL_CHAN] * value[:LOCAL_CHAN] + value[LOCAL_CHAN:] * value[LOCAL_CHAN:]
                square = power * power
                first = power if first is None else first + power
                second = square if second is None else second + square
            for kind, total in enumerate((first, second)):
                total = total + pltpu.roll(total, 64, 1)
                total = total + pltpu.roll(total, 32, 1)
                group = 2 * polar + kind
                packed = total if group == 0 else jnp.where(lane // 32 == group, total, packed)
        pltpu.make_async_copy(spectra.at[k], out_ref.at[k], leaving.at[k]).start()
        packed_ref[lax.rem(k + N_STN - me_ref[0], N_STN)] = packed
    packed_ref[N_STN] = tol_ref[...]
    for k in range(N_STN):
        pltpu.make_async_copy(spectra.at[k], out_ref.at[k], leaving.at[k]).wait()


def combine(me, own, received, tolerances):
    vmem = pl.BlockSpec(memory_space=pltpu.VMEM)
    return pl.pallas_call(
        combine_kernel,
        out_shape=[
            jax.ShapeDtypeStruct(BLOCKS, BF16),
            jax.ShapeDtypeStruct((N_STN + 1, LOCAL_CHAN, 128), F32),
        ],
        in_specs=[pl.BlockSpec(memory_space=pltpu.SMEM), vmem, vmem, vmem],
        out_specs=[pl.BlockSpec(memory_space=pltpu.HBM), vmem],
        scratch_shapes=[pltpu.VMEM(BLOCKS, BF16), pltpu.SemaphoreType.DMA((N_STN,))],
        compiler_params=pltpu.CompilerParams(vmem_limit_bytes=16 * 1024 * 1024),
        cost_estimate=pl.CostEstimate(flops=8_000_000, bytes_accessed=8_000_000, transcendentals=0),
        name="combine",
    )(me, own, received, tolerances)


STATION_ROWS = 128


def turn(offsets, number):
    unit = 2.0 * math.pi / 65536.0
    residue = (offsets * number) & 65535
    quadrant = (residue + 8192) >> 14
    angle = (residue - (quadrant << 14)).astype(F32) * unit
    square = angle * angle
    sine = angle * (1.0 + square * (-1.0 / 6.0 + square * (1.0 / 120.0 - square * (1.0 / 5040.0))))
    cosine = 1.0 + square * (
        -0.5 + square * (1.0 / 24.0 + square * (-1.0 / 720.0 + square * (1.0 / 40320.0)))
    )
    odd = (quadrant & 1) == 1
    real = jnp.where(odd, sine, cosine)
    imag = jnp.where(odd, cosine, sine)
    real = jnp.where(((quadrant + 1) & 2) == 2, -real, real)
    imag = jnp.where((quadrant & 2) == 2, -imag, imag)
    return real, imag


def times(a, b):
    return a[0] * b[0] - a[1] * b[1], a[0] * b[1] + a[1] * b[0]


def steering_kernel(start, me_ref, plan_ref, coords_ref, flags_ref, pointings_ref, out_ref, coarse, fine):
    me = me_ref[0]
    shape = (STATION_ROWS, STATIONS)
    station = pl.program_id(0) * STATION_ROWS + lax.broadcasted_iota(jnp.int32, shape, 0)
    mine = station == lax.broadcasted_iota(jnp.int32, shape, 1)

    def column(row):
        return jnp.sum(jnp.where(mine, row.astype(F32), 0.0), 1, keepdims=True)

    east = column(coords_ref[0:1, :]).astype(jnp.int32)
    north = column(coords_ref[1:2, :]).astype(jnp.int32)
    offsets = east * pointings_ref[0:1, :] + north * pointings_ref[1:2, :]
    single = turn(offsets, 1)
    pair = times(single, single)
    fine[0, 0], fine[0, 1] = single
    fine[1, 0], fine[1, 1] = pair
    for o in range(2, OWNED):
        fine[o, 0], fine[o, 1] = times((fine[o - 2, 0], fine[o - 2, 1]), pair)
    stride = (fine[OWNED - 1, 0], fine[OWNED - 1, 1])
    double = times(stride, stride)
    fast = times(double, double)
    gain = column((1 - flags_ref[...]).astype(F32) * (1.0 / math.sqrt(STATIONS)))
    gain = jnp.broadcast_to(gain, (STATION_ROWS, BEAMS))
    value = (gain, jnp.zeros_like(gain))
    if start:
        value = tuple(part * gain for part in turn(offsets, OWNED * start))
    for t in range(4):
        coarse[t, 0], coarse[t, 1] = value
        if t < 3:
            value = times(value, stride)
    for t in range(4, N_TM // 2):
        coarse[t, 0], coarse[t, 1] = times((coarse[t - 4, 0], coarse[t - 4, 1]), fast)

    def channels(n, _):
        for i in range(4):
            at = 4 * n + i
            c = at + (start and HALF)
            t, o = plan_ref[me, 3 * LOCAL_CHAN + c] - start, plan_ref[me, 4 * LOCAL_CHAN + c]
            real, imag = times((coarse[t, 0], coarse[t, 1]), (fine[o, 0], fine[o, 1]))
            out_ref[at, :, :BEAMS] = real.astype(BF16)
            out_ref[at, :, BEAMS:] = imag.astype(BF16)
        return 0

    lax.fori_loop(0, HALF // 4, channels, 0)


HALF = LOCAL_CHAN // 2


def steering(start, me, plans, coords, flags, pointings):
    smem = pl.BlockSpec(memory_space=pltpu.SMEM)
    vmem = pl.BlockSpec(memory_space=pltpu.VMEM)
    return pl.pallas_call(
        functools.partial(steering_kernel, start),
        out_shape=jax.ShapeDtypeStruct((HALF, STATIONS, 2 * BEAMS), BF16),
        grid=(STATIONS // STATION_ROWS,),
        in_specs=[smem, smem, vmem, vmem, vmem],
        out_specs=pl.BlockSpec((HALF, STATION_ROWS, 2 * BEAMS), lambda i: (0, i, 0)),
        scratch_shapes=[
            pltpu.VMEM((N_TM // 2, 2, STATION_ROWS, BEAMS), F32),
            pltpu.VMEM((OWNED, 2, STATION_ROWS, BEAMS), F32),
        ],
        compiler_params=pltpu.CompilerParams(
            dimension_semantics=("arbitrary",), vmem_limit_bytes=54 * 1024 * 1024
        ),
        cost_estimate=pl.CostEstimate(flops=40_000, bytes_accessed=12_600, transcendentals=0),
        name="steering",
    )(me, plans, coords, flags, pointings)


def place_stations(in_ref, polar, perm_ref, out_ref):
    rows = SEGS * 2 * LOCAL_CHAN
    own = slice(polar * SEGS, (polar + 1) * SEGS)
    stacked = jnp.concatenate([in_ref[g, own].reshape(rows, 128) for g in range(N_STN)], 1)
    for f4 in range(4):
        columns = slice(f4 * STATIONS, (f4 + 1) * STATIONS)
        moved = jnp.dot(stacked, perm_ref[:, columns], preferred_element_type=F32)
        for seg in range(SEGS):
            for part in range(2):
                source = (seg * 2 + part) * LOCAL_CHAN
                at = ((part * 4 + f4) * SEGS + seg) * LOCAL_CHAN
                for half in range(2):
                    piece = moved[source : source + LOCAL_CHAN, half * 128 : half * 128 + 128]
                    out_ref[half, at : at + LOCAL_CHAN, :] = piece


PLACED = (2, 32 * LOCAL_CHAN, 128)


BLOCK = 8
CHUNKS = LOCAL_CHAN // BLOCK


def beam_kernel(me_ref, plan_ref, tol_ref, *refs):
    sum_refs = refs[:N_STN]
    in_ref, perm_ref, low_ref, high_ref, out_ref = refs[N_STN : N_STN + 5]
    window_sums, ordered, first_placed, second_placed, perm, weights, powers, tolerances, softs, arrival = refs[N_STN + 5 :]

    def load(chunk):
        source, at = (low_ref, chunk) if chunk < CHUNKS // 2 else (high_ref, chunk - CHUNKS // 2)
        return pltpu.make_async_copy(
            source.at[pl.ds(at * BLOCK, BLOCK)], weights.at[pl.ds(chunk * BLOCK, BLOCK)], arrival.at[chunk]
        )

    load_perm = pltpu.make_async_copy(perm_ref, perm, arrival.at[CHUNKS])
    load_perm.start()
    for chunk in range(CHUNKS):
        load(chunk).start()
    load_perm.wait()
    place_stations(in_ref, 0, perm, first_placed)
    place_stations(in_ref, 1, perm, second_placed)
    powers[...] = jnp.zeros_like(powers)
    lane = lax.broadcasted_iota(jnp.int32, (LOCAL_CHAN, 128), 1)
    for d in range(N_STN):
        ordered[lax.rem(me_ref[0] + N_STN - d, N_STN)] = sum_refs[d][...]
    for polar in range(2):
        for kind in range(2):
            group = 2 * polar + kind
            for half in range(2):
                total = jnp.zeros((LOCAL_CHAN, 128), F32)
                for place in range(4):
                    shift = 32 * ((place - group) % 4)
                    piece = ordered[4 * half + place]
                    if shift:
                        piece = pltpu.roll(piece, shift, 1)
                    total = jnp.where(lane // 32 == place, piece, total)
                window_sums[polar, kind, :, half * 128 : half * 128 + 128] = total
    for visit in range(LOCAL_CHAN):
        tolerance = tol_ref[plan_ref[me_ref[0], visit]]
        row = pl.ds(plan_ref[me_ref[0], 2 * LOCAL_CHAN + visit], 1)
        tolerances[row, :] = jnp.full((1, STATIONS), tolerance, F32)
    size = float(WINDOW * FRAMES)
    for polar in range(2):
        s1, s2 = window_sums[polar, 0], window_sums[polar, 1]
        kurtosis = (size + 1.0) / (size - 1.0) * (size * s2 / (s1 * s1) - 1.0)
        deviation = (kurtosis - 1.0) / tolerances[...]
        softs[polar] = 1.0 / (1.0 + deviation * deviation)

    for chunk in range(CHUNKS):
        load(chunk).wait()
        for inner in range(BLOCK):
            visit = chunk * BLOCK + inner
            local = plan_ref[me_ref[0], 2 * LOCAL_CHAN + visit]
            rows = []
            for polar, ref in enumerate((first_placed, second_placed)):
                soft = softs[polar, pl.ds(local, 1), :]
                halves = [ref[half, pl.ds(local, 32, stride=LOCAL_CHAN), :] for half in range(2)]
                values = jnp.concatenate(halves, 1)
                rows.append((values * soft).astype(BF16))
            stacked = jnp.concatenate([rows[0][:16], rows[1][:16], rows[0][16:], rows[1][16:]], 0)
            product = jnp.dot(stacked, weights[visit], preferred_element_type=F32)
            real = product[:32, :BEAMS] - product[32:, BEAMS:]
            imag = product[:32, BEAMS:] + product[32:, :BEAMS]
            power = jnp.sum(real * real + imag * imag, 0, keepdims=True) * (1.0 / (2.0 * INTEG))
            powers[pl.ds(plan_ref[me_ref[0], LOCAL_CHAN + visit], 1), :] = power

    share = BEAMS // N_STN
    out_ref[...] = jnp.zeros_like(out_ref)
    for slot in range(2):
        rows = powers[slot * N_TM : (slot + 1) * N_TM, :]
        for j in range(N_STN):
            out_ref[:, j, slot * share : (slot + 1) * share] = rows[:, j * share : (j + 1) * share]


def beams(me, plans, tolerance, sums, arrived, perm, low, high):
    smem = pl.BlockSpec(memory_space=pltpu.SMEM)
    vmem = pl.BlockSpec(memory_space=pltpu.VMEM)
    low, high, perm = (pltpu.with_memory_space_constraint(x, pltpu.HBM) for x in (low, high, perm))
    return pl.pallas_call(
        beam_kernel,
        out_shape=jax.ShapeDtypeStruct((N_TM, N_STN, 128), F32),
        in_specs=[smem] * 3 + [vmem] * (N_STN + 1) + [pl.BlockSpec(memory_space=pl.ANY)] * 3,
        out_specs=vmem,
        scratch_shapes=[
            pltpu.VMEM((2, 2, LOCAL_CHAN, STATIONS), F32),
            pltpu.VMEM((N_STN, LOCAL_CHAN, 128), F32),
            pltpu.VMEM(PLACED, F32),
            pltpu.VMEM(PLACED, F32),
            pltpu.VMEM(perm.shape, BF16),
            pltpu.VMEM((LOCAL_CHAN, STATIONS, 2 * BEAMS), BF16),
            pltpu.VMEM((2 * N_TM, BEAMS), F32),
            pltpu.VMEM((LOCAL_CHAN, STATIONS), F32),
            pltpu.VMEM((2, LOCAL_CHAN, STATIONS), F32),
            pltpu.SemaphoreType.DMA((CHUNKS + 1,)),
        ],
        compiler_params=pltpu.CompilerParams(vmem_limit_bytes=36 * 1024 * 1024),
        cost_estimate=pl.CostEstimate(flops=2_400_000_000, bytes_accessed=16_000_000, transcendentals=0),
        name="beams",
    )(me, plans, tolerance, *sums, arrived, perm, low, high)


def settle_kernel(t_ref, in_ref, out_ref):
    for offset in range(OWNED):
        group = EVEN if offset in EVEN else ODD
        parity = 0 if offset in EVEN else 1
        k = 2 * lax.rem(group.index(offset) + t_ref[0], 4) + parity
        column = slot_of(offset) * 32
        out_ref[offset] = in_ref[pl.ds(k, N_TM, stride=N_STN), :][:, column : column + 32]


def settle(t, arrived):
    vmem = pl.BlockSpec(memory_space=pltpu.VMEM)
    return pl.pallas_call(
        settle_kernel,
        out_shape=jax.ShapeDtypeStruct((OWNED, N_TM, BEAMS // N_STN), F32),
        in_specs=[pl.BlockSpec(memory_space=pltpu.SMEM), vmem],
        out_specs=vmem,
        name="settle",
    )(t, arrived)


def across_stations(blocks):
    return lax.all_to_all(blocks, "stn", split_axis=0, concat_axis=0, tiled=True)


def after(value, *others):
    return lax.optimization_barrier((value, *others))[0]


def permuted(block, axis, send_to):
    return lax.ppermute(block, axis, [(i, send_to(i)) for i in range(lax.axis_size(axis))])


def window_round(sums, bits):
    parts = [permuted(sums, "tm", lambda i, flip=flip: i ^ flip) for flip in (bits[0], bits[1], bits[0] | bits[1])]
    return (sums + parts[0]) + (parts[1] + parts[2])


def per_device(voltages, taps, sk_tolerance, station_coords, pointings, station_flags):
    stn = lax.axis_index("stn")
    tm = lax.axis_index("tm")
    me = jnp.reshape(stn, (1,)).astype(jnp.int32)
    table = jnp.asarray(dft_tables())
    perm = jnp.asarray(lane_permutation())
    shift = [(i, i + 1) for i in range(N_TM - 1)]

    visited = np.array(VISITED)
    plans = np.stack([visited, np.array(VISITED_SLOTS), np.array(ORDER), visited // OWNED, visited % OWNED], 1)
    plans = jnp.asarray(plans.astype(np.int32).reshape(N_STN, 5 * LOCAL_CHAN))
    geometry = (station_coords.T, station_flags[None, :], pointings.T)

    leaving = channelize(voltages, taps, table, True)
    received = lax.ppermute(leaving, "tm", shift)
    holder = jnp.arange(CHAN, dtype=jnp.int32) // OWNED
    tolerances = jnp.where(holder == tm, jnp.tile(sk_tolerance, N_TM), 0.0)
    tolerances = jnp.pad(tolerances.reshape(CHAN // 128, 128), ((0, LOCAL_CHAN - CHAN // 128), (0, 0)))

    own = channelize(after(voltages, leaving), taps, table, False)
    blocks, sums = combine(me, own, received, tolerances)
    arrived = across_stations(blocks)
    sums = window_round(sums, (1, 2))
    low = steering(0, after(me, blocks), plans, *geometry)
    sums = window_round(after(sums, low), (4, 8))
    high = steering(N_TM // 2, after(me, low), plans, *geometry)
    sums = after(sums, high)
    tolerance = sums[N_STN, :8]
    tolerance = tolerance + permuted(tolerance, "tm", lambda i: i ^ WINDOW)
    tolerance = tolerance[: CHAN // 128].reshape(CHAN)
    window = [sums[0]] + [
        permuted(sums[d], "stn", lambda i, d=d: (i + d) % N_STN) for d in range(1, N_STN)
    ]
    outgoing = beams(me, plans, tolerance, window, arrived, perm, low, high)
    outgoing = outgoing.reshape(N_TM * N_STN, 1, 128)
    landed = lax.all_to_all(outgoing, ("tm", "stn"), split_axis=0, concat_axis=0, tiled=True)
    return settle(jnp.reshape(tm, (1,)).astype(jnp.int32), landed.reshape(N_TM * N_STN, 128))


def solution(mesh):
    in_specs = (P("tm", None, None, "stn", None), P(), P("tm"), P(), P(), P())
    out_specs = P("tm", None, "stn")
    return jax.shard_map(
        per_device, mesh=mesh, in_specs=in_specs, out_specs=out_specs, check_vma=False
    )
```
